256 devices in a mesh: blk: 32 (over z, x), span: 8 (over y, core).
Axes of the slice: x: 4, y: 4, z: 8, core: 2. Of those that a mesh axis runs over, the one named last changes fastest.
Arguments:
- fluid_adjoint_in: float32 [5, 256, 256, 128], P(None, 'blk', 'span'), may hold values from -4 to 4
- fluid_source: float32 [5, 256, 256, 128], P(None, 'blk', 'span'), may hold values from -24 to 24
- velocity: float32 [3, 256, 256, 128], P(None, 'blk', 'span'), may hold values from 0.1 to 1
- diffusion: float32 [5], replicated, may hold values from 0.5 to 2
- jacobian: float32 [5, 5], replicated, may hold values from -0.4 to 0.4
- wall_coefficient: float32 [32, 256, 128], P('blk', 'span'), may hold values from 0.5 to 2
- metal_costate_prior: float32 [512, 256, 128], P('blk', 'span'), may hold values from -4 to 4
- solid_source: float32 [512, 256, 128], P('blk', 'span'), may hold values from -12 to 12
- conductivity: float32 [512, 256, 128], P('blk', 'span'), may hold values from 0.3 to 3
- tile_owner: int32 [8, 1024, 1], P('span', 'blk'), may hold values from 0 to 31; in each aligned block of 32 rows (0 to 31, 32 to 63, ..., all dimensions but the last counted through in order) at most 3 rows name the same one
- tile_target: int32 [8, 1024], P('span', 'blk'), may hold values from 0 to 31
Outputs:
- fluid_adjoint: float32 [5, 256, 256, 128], P(None, 'blk', 'span')
- solid_adjoint: float32 [512, 256, 128], P('blk', 'span')
- residual_norms: float32 [6], replicated
The draws below stay inside these ranges and needn't reach their ends.
Inputs may be any that keep to these rules, and one draw needn't show every extreme that they name: `tile_owner`: within the 32 wall tiles of one fluid block (the rows of one device), no owner is named more than 3 times, a bound that some block reaches; every owner is named by some tile.
All inputs are finite; a program needn't handle non-finite values.
Results may differ from the reference program's by a relative error of at most 0.004.
Values sent between devices are 32-bit elements; how exact they have to be, the bound alone decides.
A program may use at most 64 MiB of HBM per device.

```python
import math
import jax
import jax.numpy as jnp
import numpy as np
from jax import lax

FIELDS = 5
CX = 8
CY = 32
AXIAL_VOLUMES = 128
CHANNEL_VOLUMES = 16
FSWEEPS = 4
SSWEEPS = 4
CAP = 3
NXF = 256
NXS = 512
RADIAL_VOLUMES = 256
N_BLK = 32
N_SPAN = 8


def place_ends(values, key, low, high):
    extent = values.shape
    index_at = [jax.random.randint(jax.random.fold_in(key, axis), (), 0, extent[axis]) for axis in range(len(extent))]
    values = values.at[tuple(index_at)].set(low)
    longest = extent.index(max(extent))
    index_at[longest] = (index_at[longest] + 1) % extent[longest]
    return values.at[tuple(index_at)].set(high)


def level_of(rng, shape, split, least, high):
    level = 1.0
    for axis_at, parts in split:
        steps = jax.random.uniform(jax.random.fold_in(jax.random.fold_in(rng, 6), axis_at), (parts,), jnp.float32, least / len(split), high / len(split))
        level = level * jnp.repeat(jnp.exp(steps), shape[axis_at] // parts).reshape((-1,) + (1,) * (len(shape) - 1 - axis_at))
    return level


def assign_block(key, own, number, rows, count, top, limit, lean):
    order = jax.random.permutation(key, count)
    heavy_load, ordinary = load_shares(count, rows * top, limit, lean, True), load_shares(count, rows * top, limit, lean, False)
    places = jnp.arange(count)

    def named(lengths, rotation):
        used = int((lengths > 0).sum())
        fixed = max(1, used // 4)
        shifted = fixed + (places - fixed + rotation * (used - fixed)) % max(1, count - fixed)
        return jnp.zeros((count,), jnp.int32).at[order[jnp.where(places < fixed, places, shifted)]].set(jnp.asarray(lengths, jnp.int32))

    lengths = jnp.where(number % 4 == 0, named(heavy_load, number // 4), named(ordinary, number - number // 4 - 1))
    mixed = jax.random.permutation(jax.random.fold_in(own, 3), count)
    source_of, receiver = mixed[0:count // 2 * 2:2], mixed[1:count // 2 * 2:2]
    margin = jnp.minimum(lengths[source_of] - 1, limit - lengths[receiver]) // 2
    margin = jnp.where((source_of == order[0]) | (receiver == order[0]) | (lengths[receiver] == 0), 0, jnp.maximum(margin, 0))
    shifted = jax.random.randint(jax.random.fold_in(own, 4), (count // 2,), 0, 1 << 20) % (margin + 1)
    lengths = lengths.at[source_of].add(-shifted).at[receiver].add(shifted)
    labels = jnp.searchsorted(jnp.cumsum(lengths), jnp.arange(rows * top), side="right").astype(jnp.int32)
    listing = labels.reshape(top, rows).T
    listing = listing[jax.random.permutation(jax.random.fold_in(own, 1), rows)]
    rotation = jax.random.randint(jax.random.fold_in(own, 2), (rows, 1), 0, top)
    return jnp.take_along_axis(listing, (jnp.arange(top)[None, :] + rotation) % top, axis=1)


def load_shares(number_of, total, limit, slope, full):
    portions = [(1 << 20) // math.isqrt(grade ** slope) + 1 for grade in range(1, number_of + 1)]
    largest = limit if full else min(limit, max(-(-total // number_of), total * portions[0] // sum(portions)))
    least = 1 if total - largest >= number_of - 1 else 0
    given, surplus = [largest] + [least] * (number_of - 1), total - largest - least * (number_of - 1)
    while surplus > 0:
        movable = [i for i in range(1, number_of) if given[i] < largest] or [i for i in range(1, number_of) if given[i] < limit]
        whole, budget = sum([portions[i] for i in movable]), surplus
        for i in movable:
            extra = min(limit - given[i], max(1, budget * portions[i] // whole), surplus)
            given[i] = given[i] + extra
            surplus = surplus - extra
    return np.array(given)


def gaussian(own_key, shape, scale, limit, split=(), kind=jnp.bfloat16):
    drawn = jax.random.normal(own_key, shape, jnp.float32) * scale
    if len(split) > 0:
        drawn = level_of(own_key, shape, split, -0.22, 0.18) * drawn
    return jnp.clip(drawn, min=-limit, max=limit).astype(kind)


def setup_inputs(seed: int = 0) -> dict:
    seeds = jax.random.split(jax.random.key(seed), 12)
    fluid_adjoint_in = gaussian(seeds[0], (FIELDS, NXF, RADIAL_VOLUMES, AXIAL_VOLUMES), 0.5, 4.0, ((1, 32), (2, 8)), jnp.float32)
    fluid_source = gaussian(seeds[1], (FIELDS, NXF, RADIAL_VOLUMES, AXIAL_VOLUMES), 4.0, 24.0, ((1, 32), (2, 8)), jnp.float32)
    velocity = jnp.clip(jnp.exp(math.log(1.0) - 2.3025851 * jax.random.uniform(seeds[2], (3, NXF, RADIAL_VOLUMES, AXIAL_VOLUMES), jnp.float32) ** level_of(seeds[2], (3, NXF, RADIAL_VOLUMES, AXIAL_VOLUMES), ((1, 32), (2, 8)), -0.2, 0.2)), 0.1, 1.0)
    diffusion = jnp.clip(jnp.exp(jax.random.uniform(seeds[3], (FIELDS,), jnp.float32, math.log(0.5), math.log(2.0))), 0.5, 2.0)
    jacobian = jnp.clip(jax.random.uniform(seeds[4], (FIELDS, FIELDS), jnp.float32, -0.4, 0.4), -0.4, 0.4)
    wall_coefficient = jnp.clip(jnp.exp(math.log(2.0) - 1.3862944 * jax.random.uniform(seeds[5], (N_BLK, RADIAL_VOLUMES, AXIAL_VOLUMES), jnp.float32) ** level_of(seeds[5], (N_BLK, RADIAL_VOLUMES, AXIAL_VOLUMES), ((0, 32), (1, 8)), -0.2, 0.2)), 0.5, 2.0)
    metal_costate_prior = gaussian(seeds[6], (NXS, RADIAL_VOLUMES, AXIAL_VOLUMES), 0.5, 4.0, ((0, 32), (1, 8)), jnp.float32)
    solid_source = gaussian(seeds[7], (NXS, RADIAL_VOLUMES, AXIAL_VOLUMES), 2.0, 12.0, ((0, 32), (1, 8)), jnp.float32)
    conductivity = jnp.clip(jnp.exp(math.log(3.0) - 2.3025851 * jax.random.uniform(seeds[8], (NXS, RADIAL_VOLUMES, AXIAL_VOLUMES), jnp.float32) ** level_of(seeds[8], (NXS, RADIAL_VOLUMES, AXIAL_VOLUMES), ((0, 32), (1, 8)), -0.2, 0.2)), 0.3, 3.0)
    tile_owner_keys = jax.random.split(jax.random.fold_in(seeds[9], 1), N_SPAN * (N_BLK * CY) // CY)
    tile_owner_turns = jax.random.permutation(jax.random.fold_in(seeds[9], 3), N_SPAN * (N_BLK * CY) // CY)
    tile_owner = jax.vmap(lambda own, number: assign_block(jax.random.fold_in(seeds[9], 2), own, number, CY, N_BLK, 1, CAP, 2))(tile_owner_keys, tile_owner_turns).reshape((N_SPAN, N_BLK * CY, 1))
    tile_target = place_ends(jax.random.randint(seeds[10], (N_SPAN, N_BLK * CY), 0, CY), jax.random.fold_in(seeds[10], 1), 0, CY - 1).astype(jnp.int32)
    return {"fluid_adjoint_in": fluid_adjoint_in, "fluid_source": fluid_source, "velocity": velocity, "diffusion": diffusion, "jacobian": jacobian, "wall_coefficient": wall_coefficient, "metal_costate_prior": metal_costate_prior, "solid_source": solid_source, "conductivity": conductivity, "tile_owner": tile_owner, "tile_target": tile_target}


damping_weight = 0.8

def fluid_operator(bordered_grid_data, velocity, spread, jacobian):
    centre = bordered_grid_data[:, 1:-1, 1:-1, 1:-1]
    x_next = bordered_grid_data[:, 2:, 1:-1, 1:-1]
    y_next = bordered_grid_data[:, 1:-1, 2:, 1:-1]
    z_next = bordered_grid_data[:, 1:-1, 1:-1, 2:]
    beside_all = x_next + bordered_grid_data[:, :-2, 1:-1, 1:-1] + y_next + bordered_grid_data[:, 1:-1, :-2, 1:-1] + z_next + bordered_grid_data[:, 1:-1, 1:-1, :-2]
    mixing = jnp.einsum('fg,gxyz->fxyz', jacobian, centre, precision=lax.Precision.HIGHEST)
    velocity_sum = velocity[0] + velocity[1] + velocity[2]
    return (6.0 * spread + velocity_sum) * centre - spread * beside_all - velocity[0] * x_next - velocity[1] * y_next - velocity[2] * z_next + mixing

def face_conductance(kappa_rim):
    centre = kappa_rim[1:-1, 1:-1, 1:-1]
    return (0.5 * (centre + kappa_rim[2:, 1:-1, 1:-1]), 0.5 * (centre + kappa_rim[:-2, 1:-1, 1:-1]), 0.5 * (centre + kappa_rim[1:-1, 2:, 1:-1]), 0.5 * (centre + kappa_rim[1:-1, :-2, 1:-1]), 0.5 * (centre + kappa_rim[1:-1, 1:-1, 2:]), 0.5 * (centre + kappa_rim[1:-1, 1:-1, :-2]))

def solid_operator(bordered_grid_data, faces, diagonal):
    centre = bordered_grid_data[1:-1, 1:-1, 1:-1]
    flows = faces[0] * bordered_grid_data[2:, 1:-1, 1:-1] + faces[1] * bordered_grid_data[:-2, 1:-1, 1:-1]
    flows = flows + faces[2] * bordered_grid_data[1:-1, 2:, 1:-1] + faces[3] * bordered_grid_data[1:-1, :-2, 1:-1]
    flows = flows + faces[4] * bordered_grid_data[1:-1, 1:-1, 2:] + faces[5] * bordered_grid_data[1:-1, 1:-1, :-2]
    return diagonal * centre - flows

def reference(fluid_adjoint_in, fluid_source, velocity, diffusion, jacobian, wall_coefficient, metal_costate_prior, solid_source, conductivity, tile_owner, tile_target):
    spread = diffusion[:, None, None, None]
    fluid_diagonal = 6.0 * spread + (velocity[0] + velocity[1] + velocity[2]) + jnp.diagonal(jacobian)[:, None, None, None]
    adjoint = fluid_adjoint_in
    for iteration in range(FSWEEPS):
        bordered_grid_data = jnp.pad(adjoint, ((0, 0), (1, 1), (1, 1), (1, 1)))
        fluid_residual = fluid_source - fluid_operator(bordered_grid_data, velocity, spread, jacobian)
        adjoint = adjoint + damping_weight * fluid_residual / fluid_diagonal
    owner = tile_owner[:, :, 0].reshape(N_SPAN, N_BLK, CY).transpose(1, 0, 2).reshape(N_BLK, RADIAL_VOLUMES).astype(jnp.int32)
    target = tile_target.reshape(N_SPAN, N_BLK, CY).transpose(1, 0, 2).reshape(N_BLK, RADIAL_VOLUMES).astype(jnp.int32)
    row_base = (jnp.arange(RADIAL_VOLUMES, dtype=jnp.int32) // CY * CY).astype(jnp.int32)
    destination_rank = (owner * RADIAL_VOLUMES + row_base[None, :] + target).reshape(-1).astype(jnp.int32)
    wall_flux = wall_coefficient * adjoint[4, ::CX]
    surface = jax.ops.segment_sum(wall_flux.reshape(N_BLK * RADIAL_VOLUMES, AXIAL_VOLUMES), destination_rank, num_segments=N_BLK * RADIAL_VOLUMES).reshape(N_BLK, RADIAL_VOLUMES, AXIAL_VOLUMES)
    heat_source = solid_source.at[CHANNEL_VOLUMES - 1::CHANNEL_VOLUMES].add(surface)
    kappa_rim = jnp.pad(conductivity, 1)
    faces = face_conductance(kappa_rim)
    metal_pivot_entries = faces[0] + faces[1] + faces[2] + faces[3] + faces[4] + faces[5]
    thermal_state_grid = metal_costate_prior
    for iteration in range(SSWEEPS):
        bordered_grid_data = jnp.pad(thermal_state_grid, 1)
        metal_imbalance_grid = heat_source - solid_operator(bordered_grid_data, faces, metal_pivot_entries)
        thermal_state_grid = thermal_state_grid + damping_weight * metal_imbalance_grid / metal_pivot_entries
    interface_heat_level = thermal_state_grid[CHANNEL_VOLUMES - 1::CHANNEL_VOLUMES].reshape(N_BLK * RADIAL_VOLUMES, AXIAL_VOLUMES)
    output_entries = jnp.take(interface_heat_level, destination_rank, axis=0).reshape(N_BLK, RADIAL_VOLUMES, AXIAL_VOLUMES)
    gas_outcome = adjoint.at[4, ::CX].add(wall_coefficient * output_entries)
    squares = jnp.concatenate([lax.optimization_barrier(jnp.sum(fluid_residual * fluid_residual, axis=(1, 2, 3))), jnp.sum(metal_imbalance_grid * metal_imbalance_grid)[None]])
    fluid_cells = float(NXF * RADIAL_VOLUMES * AXIAL_VOLUMES)
    solid_cells = float(NXS * RADIAL_VOLUMES * AXIAL_VOLUMES)
    counts = jnp.array([fluid_cells] * 5 + [solid_cells], jnp.float32)
    magnitude_list = jnp.sqrt(squares / counts)
    return (gas_outcome, thermal_state_grid, magnitude_list)
```

```python
import functools

import jax
import jax.numpy as jnp
from jax import lax
from jax.experimental import pallas as pl
from jax.experimental.pallas import tpu as pltpu
from jax.sharding import PartitionSpec as P

MESH = pl.DeviceIdType.MESH
F32 = jnp.float32
NF = 5
CX = 8
CY = 32
CH = 16
NZ = 128
ROWS = 48
O = 8
W4 = 4
SWEEPS = 4
OMEGA = 0.8


def kernel(
    nb,
    nsp,
    slot,
    fluid_cells,
    solid_cells,
    adj_in,
    src_in,
    vel_in,
    dif,
    jac,
    wall_in,
    tem_in,
    heat_in,
    con_in,
    owner_in,
    target_in,
    adj_out,
    sol_out,
    norm_out,
    adj,
    src,
    vel,
    inv,
    wall,
    fin,
    tem,
    con,
    heat,
    sgz,
    sd2,
    sdi,
    tout,
    r0,
    r0_up,
    kc,
    cgz,
    cd2,
    cdi,
    hc,
    dl,
    dup,
    dlow,
    pmat,
    pmat_t,
    smat,
    smat_t,
    msend,
    mrecv,
    fsend,
    frecv,
    rsend,
    rrecv,
    nsend,
    nrecv,
    lsem,
    osem,
    fs,
    fr,
    ts,
    tr,
    ks,
    kr,
    xs,
    xr,
    as_,
    ar,
):
    ns = nb * slot
    mb = lax.axis_index("blk")
    ms = lax.axis_index("span")
    has_lo_b, has_hi_b = mb > 0, mb < nb - 1
    has_lo_s, has_hi_s = ms > 0, ms < nsp - 1
    lo_b, hi_b = {"blk": mb - 1}, {"blk": mb + 1}
    lo_s, hi_s = {"span": ms - 1}, {"span": ms + 1}
    has = (has_hi_b, has_lo_b, has_hi_s, has_lo_s)
    came = (has_lo_b, has_hi_b, has_lo_s, has_hi_s)
    peer = (hi_b, lo_b, hi_s, lo_s)

    own = pl.ds(O, CY)

    barrier = pltpu.get_barrier_semaphore()

    def far_first(k, n):
        step = (k + 1) // 2
        return n // 2 + jnp.where(lax.rem(k, 2) == 1, step, -step)

    @pl.loop(0, nb - 1)
    def _(k):
        pl.semaphore_signal(
            barrier, inc=1, device_id={"blk": lax.rem(mb + far_first(k, nb), nb)}, device_id_type=MESH
        )

    @pl.loop(1, nsp)
    def _(k):
        pl.semaphore_signal(barrier, inc=1, device_id={"span": lax.rem(ms + k, nsp)}, device_id_type=MESH)

    loads = [
        pltpu.make_async_copy(adj_in, adj.at[0, :, pl.ds(1, CX), own, :], lsem.at[0]),
        pltpu.make_async_copy(vel_in, vel, lsem.at[1]),
        pltpu.make_async_copy(src_in, src, lsem.at[2]),
        pltpu.make_async_copy(con_in, con.at[pl.ds(1, CH), own, :], lsem.at[3]),
        pltpu.make_async_copy(tem_in, tem.at[0, pl.ds(1, CH), own, :], lsem.at[4]),
        pltpu.make_async_copy(heat_in, heat, lsem.at[5]),
        pltpu.make_async_copy(wall_in.at[0], wall, lsem.at[6]),
    ]
    for copy in loads:
        copy.start()

    def zero_halos(cond, put):
        @pl.when(jnp.logical_not(cond))
        def _():
            put()

    def z_lo_b():
        for e in range(SWEEPS):
            adj[e, :, 0, O : O + CY, :] = jnp.zeros((NF, CY, NZ), F32)
            tem[e, 0, O : O + CY, :] = jnp.zeros((CY, NZ), F32)
        con[0, O : O + CY, :] = jnp.zeros((CY, NZ), F32)
        dlow[...] = jnp.zeros_like(dlow)

    def z_hi_b():
        for e in range(SWEEPS):
            adj[e, :, CX + 1, O : O + CY, :] = jnp.zeros((NF, CY, NZ), F32)
            tem[e, CH + 1, O : O + CY, :] = jnp.zeros((CY, NZ), F32)
        con[CH + 1, O : O + CY, :] = jnp.zeros((CY, NZ), F32)
        kc[5:9, O - W4 : O + CY + W4, :] = jnp.zeros((4, CY + 2 * W4, NZ), F32)
        r0_up[...] = jnp.zeros_like(r0_up)

    def z_span(halo, wide):
        def put():
            for e in range(SWEEPS):
                adj[e, :, 1 : CX + 1, halo : halo + 1, :] = jnp.zeros((NF, CX, 1, NZ), F32)
                tem[e, 1 : CH + 1, halo : halo + 1, :] = jnp.zeros((CH, 1, NZ), F32)
            con[1 : CH + 1, wide : wide + W4, :] = jnp.zeros((CH, W4, NZ), F32)
            hc[4, wide : wide + W4, :] = jnp.zeros((W4, NZ), F32)

        return put

    zero_halos(has_lo_b, z_lo_b)
    zero_halos(has_hi_b, z_hi_b)
    zero_halos(has_lo_s, z_span(O - 1, O - W4))
    zero_halos(has_hi_s, z_span(O + CY, O + CY))

    pl.semaphore_wait(barrier, nb - 1 + nsp - 1)

    def fluid_copy(e, d, first=False):
        if d < 2:
            plane = (CX, 1)[d]
            source = adj_in.at[:, plane - 1] if first else adj.at[e, :, plane, own, :]
            dest = adj.at[e, :, (0, CX + 1)[d], own, :]
        else:
            row = (CY - 1, 0)[d - 2]
            source = (
                adj_in.at[:, :, pl.ds(row, 1), :]
                if first
                else adj.at[e, :, pl.ds(1, CX), pl.ds(O + row, 1), :]
            )
            dest = adj.at[e, :, pl.ds(1, CX), pl.ds((O - 1, O + CY)[d - 2], 1), :]
        return pltpu.make_async_remote_copy(
            source, dest, fs.at[e, d], fr.at[e, d], device_id=peer[d], device_id_type=MESH
        )

    def solid_copy(e, d, first=False):
        if d < 2:
            plane = (CH, 1)[d]
            source = tem_in.at[plane - 1] if first else tem.at[e, plane, own, :]
            dest = tem.at[e, (0, CH + 1)[d], own, :]
        else:
            row = (CY - 1, 0)[d - 2]
            source = (
                tem_in.at[:, pl.ds(row, 1), :]
                if first
                else tem.at[e, pl.ds(1, CH), pl.ds(O + row, 1), :]
            )
            dest = tem.at[e, pl.ds(1, CH), pl.ds((O - 1, O + CY)[d - 2], 1), :]
        return pltpu.make_async_remote_copy(
            source, dest, ts.at[e, d], tr.at[e, d], device_id=peer[d], device_id_type=MESH
        )

    def con_copy(d):
        if d < 2:
            source = con_in.at[(CH - 1, 0)[d]]
            dest = con.at[(0, CH + 1)[d], own, :]
        else:
            source = con_in.at[:, pl.ds((CY - W4, 0)[d - 2], W4), :]
            dest = con.at[pl.ds(1, CH), pl.ds((O - W4, O + CY)[d - 2], W4), :]
        return pltpu.make_async_remote_copy(
            source, dest, ks.at[d], kr.at[d], device_id=peer[d], device_id_type=MESH
        )

    wide_rows = pl.ds(O - W4, CY + 2 * W4)
    wide_copy = pltpu.make_async_remote_copy(
        con.at[pl.ds(1, 4), wide_rows, :],
        kc.at[pl.ds(5, 4), wide_rows, :],
        ks.at[4],
        kr.at[4],
        device_id=lo_b,
        device_id_type=MESH,
    )
    r0_copy = pltpu.make_async_remote_copy(
        r0.at[pl.ds(0, 3)], r0_up, ks.at[5], kr.at[5], device_id=lo_b, device_id_type=MESH
    )
    dl_copy = pltpu.make_async_remote_copy(
        dup, dlow, ks.at[6], kr.at[6], device_id=hi_b, device_id_type=MESH
    )

    def edge_copy(d):
        source = hc.at[4, pl.ds((O + CY - W4, O)[d - 2], W4), :]
        dest = hc.at[4, pl.ds((O - W4, O + CY)[d - 2], W4), :]
        return pltpu.make_async_remote_copy(
            source, dest, ks.at[5 + d], kr.at[5 + d], device_id=peer[d], device_id_type=MESH
        )

    def go(cond, copy):
        @pl.when(cond)
        def _():
            copy.start()

    def arrived(cond, copy):
        @pl.when(cond)
        def _():
            copy.wait_recv()

    def left(cond, copy):
        @pl.when(cond)
        def _():
            copy.wait_send()

    def spread(send, recv, sem):
        @pl.loop(0, nb - 1)
        def _(k):
            to = lax.rem(mb + far_first(k, nb), nb)
            pltpu.make_async_remote_copy(
                send.at[pl.ds(to * slot, slot), :],
                recv.at[pl.ds(mb * slot, slot), :],
                as_.at[sem],
                ar.at[sem],
                device_id={"blk": to},
                device_id_type=MESH,
            ).start()

    def spread_waiter(send, recv, sem):
        rows = pl.ds(0, (nb - 1) * slot)
        return pltpu.make_async_remote_copy(
            send.at[rows, :], recv.at[rows, :], as_.at[sem], ar.at[sem], device_id=hi_b, device_id_type=MESH
        )

    for d in range(4):
        go(has[d], fluid_copy(0, d, True))
    for d in range(4):
        go(has[d], con_copy(d))
    for d in range(4):
        go(has[d], solid_copy(0, d, True))

    own_block = pl.ds(mb * slot, slot)
    ow = owner_in[...].astype(F32)
    tg = target_in[...].astype(F32)
    rows2 = lax.broadcasted_iota(jnp.int32, (CY, CY), 0)
    cols2 = lax.broadcasted_iota(jnp.int32, (CY, CY), 1)
    ow_l = jnp.broadcast_to(ow, (CY, CY))
    ow_s = jnp.sum(jnp.where(rows2 == cols2, ow_l, 0.0), axis=1, keepdims=True)
    same = jnp.where(jnp.broadcast_to(ow_s, (CY, CY)) == ow_l, 1.0, 0.0)
    rank_l = jnp.sum(jnp.where(rows2 < cols2, same, 0.0), axis=0, keepdims=True)
    rank_s = jnp.sum(jnp.where(cols2 < rows2, same, 0.0), axis=1, keepdims=True)
    slot_l = ow * float(slot) + rank_l
    slot_s = ow_s * float(slot) + rank_s
    p_rows = lax.broadcasted_iota(jnp.int32, (ns, CY), 0).astype(F32)
    hot = jnp.broadcast_to(slot_l, (ns, CY)) == p_rows
    pmat[...] = jnp.where(hot, 1.0, 0.0)
    p_cols = lax.broadcasted_iota(jnp.int32, (CY, ns), 1).astype(F32)
    pmat_t[...] = jnp.where(jnp.broadcast_to(slot_s, (CY, ns)) == p_cols, 1.0, 0.0)
    meta = jnp.sum(jnp.where(hot, jnp.broadcast_to(tg + 1.0, (ns, CY)), 0.0), axis=1, keepdims=True) - 1.0
    msend[...] = jnp.broadcast_to(meta, (ns, NZ))
    spread(msend, mrecv, 0)
    mrecv[own_block, :] = msend[own_block, :]

    lane = lax.broadcasted_iota(jnp.int32, (CY, NZ), 1)
    first_lane, last_lane = lane == 0, lane == NZ - 1

    loads[1].wait()

    @pl.loop(0, CX)
    def _(x):
        total = vel[0, x] + vel[1, x] + vel[2, x]
        for f in range(NF):
            inv[f, x] = OMEGA / (total + (6.0 * dif[f] + jac[f, f]))

    for k in range(3):
        dl[k] = jnp.zeros((9, ROWS, NZ), F32)
    for p in range(9):
        if p != 4:
            hc[p] = jnp.zeros((ROWS, NZ), F32)
        kc[p, 0 : O - W4, :] = jnp.zeros((O - W4, NZ), F32)
        kc[p, O + CY + W4 : ROWS, :] = jnp.zeros((ROWS - O - CY - W4, NZ), F32)
    hc[4, 0 : O - W4, :] = jnp.zeros((O - W4, NZ), F32)
    hc[4, O + CY + W4 : ROWS, :] = jnp.zeros((ROWS - O - CY - W4, NZ), F32)

    def fluid_plane(e, x):
        centre = [adj[e, f, x, O : O + CY, :] for f in range(NF)]
        u = [vel[i, x - 1] for i in range(3)]
        total = u[0] + u[1] + u[2]
        squares = []
        for f in range(NF):
            c, d = centre[f], dif[f]
            x_next = adj[e, f, x + 1, O : O + CY, :]
            y_next = adj[e, f, x, O + 1 : O + 1 + CY, :]
            z_next = jnp.where(last_lane, 0.0, pltpu.roll(c, NZ - 1, 1))
            back = (
                adj[e, f, x - 1, O : O + CY, :]
                + adj[e, f, x, O - 1 : O - 1 + CY, :]
                + jnp.where(first_lane, 0.0, pltpu.roll(c, 1, 1))
            )
            residual = src[f, x - 1] - (6.0 * d + total) * c + d * back
            residual = residual + (d + u[0]) * x_next + (d + u[1]) * y_next + (d + u[2]) * z_next
            mixing = jac[f, 0] * centre[0]
            for g in range(1, NF):
                mixing = mixing + jac[f, g] * centre[g]
            residual = residual - mixing
            adj[e + 1, f, x, O : O + CY, :] = c + inv[f, x - 1] * residual
            squares.append(residual)
        return squares

    def folded(values):
        return (values * values).reshape(CY // 8, 8, NZ).sum(axis=0)

    def flows2(q, k, gz, i, a, n):
        c, kk = q[i, pl.ds(a, n), :], k[i, pl.ds(a, n), :]
        flow = (kk + k[i + 1, pl.ds(a, n), :]) * q[i + 1, pl.ds(a, n), :]
        flow = flow + (kk + k[i - 1, pl.ds(a, n), :]) * q[i - 1, pl.ds(a, n), :]
        flow = flow + (kk + k[i, pl.ds(a + 1, n), :]) * q[i, pl.ds(a + 1, n), :]
        flow = flow + (kk + k[i, pl.ds(a - 1, n), :]) * q[i, pl.ds(a - 1, n), :]
        flow = flow + gz * pltpu.roll(c, NZ - 1, 1) + pltpu.roll(gz * c, 1, 1)
        return c, flow

    def coefficients(k, i, a, n):
        kk = k[i, pl.ds(a, n), :]
        at = lax.broadcasted_iota(jnp.int32, (n, NZ), 1)
        k_next = jnp.where(at == NZ - 1, 0.0, pltpu.roll(kk, NZ - 1, 1))
        k_back = jnp.where(at == 0, 0.0, pltpu.roll(kk, 1, 1))
        diagonal = 6.0 * kk + k[i + 1, pl.ds(a, n), :] + k[i - 1, pl.ds(a, n), :]
        diagonal = diagonal + k[i, pl.ds(a + 1, n), :] + k[i, pl.ds(a - 1, n), :] + k_next + k_back
        gz = jnp.where(at == NZ - 1, 0.0, kk + k_next)
        return gz, diagonal

    def solid_plane(e, p):
        c, flow = flows2(tem.at[e], con, sgz[p - 1], p, O, CY)
        residual = heat[p - 1] - 0.5 * (sd2[p - 1] * c - flow)
        return residual, c + sdi[p - 1] * residual

    def solid_prepare():
        loads[3].wait()
        for d in range(4):
            arrived(came[d], con_copy(d))

        @pl.loop(1, CH + 1)
        def _(p):
            gz, diagonal = coefficients(con, p, O, CY)
            sgz[p - 1] = gz
            sd2[p - 1] = diagonal
            sdi[p - 1] = (2.0 * OMEGA) / diagonal

    def solid_wait(e):
        for d in range(4):
            arrived(came[d], solid_copy(e, d, e == 0))

    def solid_sweep(e):
        def put(p):
            tem[e + 1, p, O : O + CY, :] = solid_plane(e, p)[1]

        put(1)
        put(CH)
        for d in range(2):
            go(has[d], solid_copy(e + 1, d))

        @pl.loop(2, CH)
        def _(p):
            put(p)

        for d in range(2, 4):
            go(has[d], solid_copy(e + 1, d))

    loads[0].wait()
    loads[2].wait()
    for e in range(SWEEPS - 1):
        for d in range(4):
            arrived(came[d], fluid_copy(e, d, e == 0))

        @pl.loop(0, 2)
        def _(i):
            fluid_plane(e, 1 + i * (CX - 1))

        for d in range(2):
            go(has[d], fluid_copy(e + 1, d))

        @pl.loop(2, CX)
        def _(x):
            fluid_plane(e, x)

        for d in range(2, 4):
            go(has[d], fluid_copy(e + 1, d))
        if e == 0:
            solid_prepare()
            loads[4].wait()
            loads[5].wait()
        if e == SWEEPS - 2:
            go(has_lo_b, wide_copy)
        solid_wait(e)
        solid_sweep(e)

    n40 = CY + 2 * W4
    for p in range(5):
        kc[p, O - W4 : O + CY + W4, :] = con[12 + p, O - W4 : O + CY + W4, :]

    spread_waiter(msend, mrecv, 0).wait_recv()
    hit = jnp.where(
        mrecv[...] == lax.broadcasted_iota(jnp.int32, (ns, NZ), 1).astype(F32), 1.0, 0.0
    )
    smat_t[...] = hit
    smat[...] = jnp.transpose(hit)
    loads[6].wait()

    e = SWEEPS - 1
    for d in range(4):
        arrived(came[d], fluid_copy(e, d))
    squares = [folded(r) for r in fluid_plane(e, 1)]
    flux = wall[...] * adj[SWEEPS, NF - 1, 1, O : O + CY, :]
    fsend[...] = jnp.dot(pmat[...], flux, precision=lax.Precision.HIGHEST, preferred_element_type=F32)
    spread(fsend, frecv, 1)
    frecv[own_block, :] = fsend[own_block, :]

    def more(x, carry):
        return tuple(a + folded(r) for a, r in zip(carry, fluid_plane(e, x)))

    squares = lax.fori_loop(2, CX + 1, more, tuple(squares))
    outs = [
        pltpu.make_async_copy(
            adj.at[SWEEPS, pl.ds(0, NF - 1), pl.ds(1, CX), own, :], adj_out.at[pl.ds(0, NF - 1)], osem.at[0]
        ),
        pltpu.make_async_copy(
            adj.at[SWEEPS, NF - 1, pl.ds(2, CX - 1), own, :], adj_out.at[NF - 1, pl.ds(1, CX - 1)], osem.at[1]
        ),
    ]
    for copy in outs:
        copy.start()

    solid_wait(e)
    zero8 = jnp.zeros((8, NZ), F32)

    def edge(first, count, at):
        def body(i, carry):
            residual, new = solid_plane(e, first + i)
            tout[first + i - 1] = new
            r0[at + i] = residual
            return carry + folded(residual)

        return lax.fori_loop(0, count, body, zero8)

    low_squares = edge(1, 3, 0)
    go(has_lo_b, r0_copy)
    edge(13, 4, 3)

    def middle(p, carry):
        residual, new = solid_plane(e, p)
        tout[p - 1] = new
        return carry + folded(residual)

    solid_squares = lax.fori_loop(4, 13, middle, zero8)
    outs.append(pltpu.make_async_copy(tout.at[pl.ds(3, 9)], sol_out.at[pl.ds(3, 9)], osem.at[2]))
    outs[-1].start()
    solid_squares = solid_squares + jnp.where(has_lo_b, 0.0, low_squares)

    arrived(has_hi_b, wide_copy)
    row = lax.broadcasted_iota(jnp.int32, (n40, NZ), 0) - W4
    inside = (row >= jnp.where(has_lo_s, -3, 0)) & (row <= jnp.where(has_hi_s, CY + 2, CY - 1))

    @pl.loop(1, 8)
    def _(i):
        gz, diagonal = coefficients(kc, i, O - W4, n40)
        ok = inside & ((i < 5) | has_hi_b)
        cgz[i] = gz
        cd2[i] = diagonal
        cdi[i] = jnp.where(ok, (2.0 * OMEGA) / jnp.where(ok, diagonal, 1.0), 0.0)

    lane8 = lax.broadcasted_iota(jnp.int32, (8, NZ), 1)
    row8 = lax.broadcasted_iota(jnp.int32, (8, NZ), 0)
    sums = jnp.zeros((8, NZ), F32)
    for f in range(NF):
        sums = sums + jnp.where(row8 == f, jnp.broadcast_to(jnp.sum(squares[f], axis=0, keepdims=True), (8, NZ)), 0.0)

    spread_waiter(fsend, frecv, 1).wait_recv()
    surface = jnp.dot(smat[0:CY, :], frecv[...], precision=lax.Precision.HIGHEST, preferred_element_type=F32)
    hc[4, O : O + CY, :] = surface
    for d in (2, 3):
        go(has[d], edge_copy(d))
    for d in (2, 3):
        arrived(came[d], edge_copy(d))
    arrived(has_hi_b, r0_copy)

    wide = slice(O - W4, O + CY + W4)
    dl[0, 4, wide, :] = cdi[4] * hc[4, wide, :]
    for k in range(2):

        @pl.loop(3 - k, 6 + k)
        def _(i):
            c, flow = flows2(dl.at[k], kc, cgz[i], i, O - W4, n40)
            dl[k + 1, i, wide, :] = c + cdi[i] * (hc[i, wide, :] - 0.5 * (cd2[i] * c - flow))

    mid = pl.ds(W4, CY)

    def last(i):
        c, flow = flows2(dl.at[2], kc, cgz[i, mid, :], i, O, CY)
        residual = hc[i, O : O + CY, :] - 0.5 * (cd2[i, mid, :] * c - flow)
        return residual, c + cdi[i, mid, :] * residual

    def last_own(i, carry):
        residual, delta = last(i)
        tout[11 + i] = tout[11 + i] + delta
        return carry + folded(residual + r0[2 + i])

    solid_squares = lax.fori_loop(1, 5, last_own, solid_squares)

    def last_up(i, carry):
        residual, delta = last(i)
        dup[i - 5] = delta
        return carry + folded(residual + r0_up[i - 5])

    up_squares = lax.fori_loop(5, 8, last_up, zero8)
    go(has_hi_b, dl_copy)
    solid_squares = solid_squares + jnp.where(has_hi_b, up_squares, 0.0)
    sums = sums + jnp.where(row8 == NF, jnp.broadcast_to(jnp.sum(solid_squares, axis=0, keepdims=True), (8, NZ)), 0.0)
    totals = jnp.broadcast_to(jnp.sum(sums, axis=1, keepdims=True), (8, NZ))
    totals = jnp.sum(jnp.where(row8 == lane8, totals, 0.0), axis=0, keepdims=True)

    back = jnp.dot(smat_t[:, 0:CY], tout[CH - 1], precision=lax.Precision.HIGHEST, preferred_element_type=F32)
    free = lax.rem(lax.broadcasted_iota(jnp.int32, (ns, NZ), 0), slot) == slot - 1
    rsend[...] = jnp.where(free, jnp.broadcast_to(totals, (ns, NZ)), back)
    spread(rsend, rrecv, 2)
    rrecv[own_block, :] = rsend[own_block, :]
    outs.append(pltpu.make_async_copy(tout.at[pl.ds(12, 4)], sol_out.at[pl.ds(12, 4)], osem.at[3]))
    outs[-1].start()

    arrived(has_lo_b, dl_copy)
    for i in range(3):
        tout[i] = tout[i] + dlow[i]
    outs.append(pltpu.make_async_copy(tout.at[pl.ds(0, 3)], sol_out.at[pl.ds(0, 3)], osem.at[4]))
    outs[-1].start()

    spread_waiter(rsend, rrecv, 2).wait_recv()
    got = rrecv[...]
    nsend[...] = jnp.sum(jnp.where(free, got, 0.0), axis=0, keepdims=True)

    def norm_copy(to):
        return pltpu.make_async_remote_copy(
            nsend, nrecv.at[ms], as_.at[3], ar.at[3], device_id={"span": to}, device_id_type=MESH
        )

    @pl.loop(1, nsp)
    def _(k):
        norm_copy(lax.rem(ms + k, nsp)).start()

    nrecv[ms] = nsend[...]
    returned = jnp.dot(pmat_t[...], got, precision=lax.Precision.HIGHEST, preferred_element_type=F32)
    fin[...] = adj[SWEEPS, NF - 1, 1, O : O + CY, :] + wall[...] * returned
    outs.append(pltpu.make_async_copy(fin, adj_out.at[NF - 1, 0], osem.at[5]))
    outs[-1].start()

    norm_waiter = pltpu.make_async_remote_copy(
        nrecv.at[pl.ds(0, nsp - 1)],
        nrecv.at[pl.ds(0, nsp - 1)],
        as_.at[3],
        ar.at[3],
        device_id=hi_s,
        device_id_type=MESH,
    )
    norm_waiter.wait_recv()
    total = nrecv[0]
    for k in range(1, nsp):
        total = total + nrecv[k]
    cells = jnp.where(lane8 < NF, fluid_cells, solid_cells)
    norm_out[...] = jnp.sqrt(jnp.broadcast_to(total, (8, NZ)) / cells)

    for e in range(SWEEPS):
        for d in range(4):
            left(has[d], fluid_copy(e, d, e == 0))
            left(has[d], solid_copy(e, d, e == 0))
    for d in range(4):
        left(has[d], con_copy(d))
    left(has_lo_b, wide_copy)
    left(has_lo_b, r0_copy)
    left(has_hi_b, dl_copy)
    for d in (2, 3):
        left(has[d], edge_copy(d))
    spread_waiter(msend, mrecv, 0).wait_send()
    spread_waiter(fsend, frecv, 1).wait_send()
    spread_waiter(rsend, rrecv, 2).wait_send()
    norm_waiter.wait_send()
    for copy in outs:
        copy.wait()


def shards(
    nb,
    nsp,
    slot,
    fluid_adjoint_in,
    fluid_source,
    velocity,
    diffusion,
    jacobian,
    wall_coefficient,
    metal_costate_prior,
    solid_source,
    conductivity,
    tile_owner,
    tile_target,
):
    ns = nb * slot
    every = nb * nsp
    anywhere = pl.BlockSpec(memory_space=pl.ANY)
    vmem = pl.BlockSpec(memory_space=pltpu.VMEM)
    smem = pl.BlockSpec(memory_space=pltpu.SMEM)
    V = pltpu.VMEM
    n40 = CY + 2 * W4
    dma = pltpu.SemaphoreType.DMA
    scratch = [
        V((SWEEPS + 1, NF, CX + 2, ROWS, NZ), F32),
        V((NF, CX, CY, NZ), F32),
        V((3, CX, CY, NZ), F32),
        V((NF, CX, CY, NZ), F32),
        V((CY, NZ), F32),
        V((CY, NZ), F32),
        V((SWEEPS, CH + 2, ROWS, NZ), F32),
        V((CH + 2, ROWS, NZ), F32),
        V((CH, CY, NZ), F32),
        V((CH, CY, NZ), F32),
        V((CH, CY, NZ), F32),
        V((CH, CY, NZ), F32),
        V((CH, CY, NZ), F32),
        V((7, CY, NZ), F32),
        V((3, CY, NZ), F32),
        V((9, ROWS, NZ), F32),
        V((8, n40, NZ), F32),
        V((8, n40, NZ), F32),
        V((8, n40, NZ), F32),
        V((9, ROWS, NZ), F32),
        V((3, 9, ROWS, NZ), F32),
        V((3, CY, NZ), F32),
        V((3, CY, NZ), F32),
        V((ns, CY), F32),
        V((CY, ns), F32),
        V((NZ, ns), F32),
        V((ns, NZ), F32),
    ]
    scratch += [V((ns, NZ), F32)] * 6
    scratch += [V((1, NZ), F32), V((nsp, 1, NZ), F32)]
    scratch += [
        dma((7,)),
        dma((6,)),
        dma((SWEEPS, 4)),
        dma((SWEEPS, 4)),
        dma((SWEEPS, 4)),
        dma((SWEEPS, 4)),
        dma((9,)),
        dma((9,)),
        dma((1,)),
        dma((1,)),
        dma((4,)),
        dma((4,)),
    ]
    adjoint, solid, norms = pl.pallas_call(
        functools.partial(
            kernel, nb, nsp, slot, float(CX * CY * NZ * every), float(CH * CY * NZ * every)
        ),
        out_shape=(
            jax.ShapeDtypeStruct(fluid_adjoint_in.shape, F32),
            jax.ShapeDtypeStruct(metal_costate_prior.shape, F32),
            jax.ShapeDtypeStruct((8, NZ), F32),
        ),
        in_specs=[anywhere, anywhere, anywhere, smem, smem, anywhere, anywhere, anywhere, anywhere, vmem, vmem],
        out_specs=(anywhere, anywhere, vmem),
        scratch_shapes=scratch,
        compiler_params=pltpu.CompilerParams(collective_id=0, has_side_effects=True),
        name="iteration",
    )(
        fluid_adjoint_in,
        fluid_source,
        velocity,
        diffusion,
        jacobian,
        wall_coefficient,
        metal_costate_prior,
        solid_source,
        conductivity,
        tile_owner.reshape(1, CY),
        tile_target,
    )
    return adjoint, solid, norms[0, : NF + 1]


def solution(mesh, slot=4):
    placed = (
        P(None, "blk", "span", None),
        P(None, "blk", "span", None),
        P(None, "blk", "span", None),
        P(),
        P(),
        P("blk", "span", None),
        P("blk", "span", None),
        P("blk", "span", None),
        P("blk", "span", None),
        P("span", "blk", None),
        P("span", "blk"),
    )
    return jax.shard_map(
        functools.partial(shards, mesh.shape["blk"], mesh.shape["span"], slot),
        mesh=mesh,
        in_specs=placed,
        out_specs=(P(None, "blk", "span", None), P("blk", "span", None), P()),
        check_vma=False,
    )
```

```python
import functools

import jax
import jax.numpy as jnp
from jax import lax
from jax.experimental import pallas as pl
from jax.experimental.pallas import tpu as pltpu
from jax.sharding import PartitionSpec as P

MESH = pl.DeviceIdType.MESH
F32 = jnp.float32
NF = 5
CX = 8
CY = 32
CH = 16
NZ = 128
ROWS = 48
O = 8
W4 = 4
SWEEPS = 4
OMEGA = 0.8


def kernel(
    nb,
    nsp,
    slot,
    fluid_cells,
    solid_cells,
    adj_in,
    src_in,
    vel_in,
    dif_in,
    jac_in,
    wall_in,
    tem_in,
    heat_in,
    con_in,
    owner_in,
    target_in,
    adj_out,
    sol_out,
    norm_out,
    dif,
    jac,
    owner_v,
    target_v,
    adj,
    src,
    vel,
    inv,
    wall,
    fin,
    tem,
    con,
    heat,
    sgz,
    sd2,
    sdi,
    tout,
    r0,
    r0_up,
    kc,
    cgz,
    cd2,
    cdi,
    hc,
    dl,
    dup,
    dlow,
    pmat,
    pmat_t,
    smat,
    smat_t,
    msend,
    mrecv,
    fsend,
    frecv,
    rsend,
    rrecv,
    nsend,
    nrecv,
    lsem,
    osem,
    fs,
    fr,
    ts,
    tr,
    ks,
    kr,
    xs,
    xr,
    as_,
    ar,
    ws,
    wr,
    gb,
    gs,
):
    ns = nb * slot
    mb = lax.axis_index("blk")
    ms = lax.axis_index("span")
    has_lo_b, has_hi_b = mb > 0, mb < nb - 1
    has_lo_s, has_hi_s = ms > 0, ms < nsp - 1
    lo_b, hi_b = {"blk": mb - 1}, {"blk": mb + 1}
    lo_s, hi_s = {"span": ms - 1}, {"span": ms + 1}
    has = (has_hi_b, has_lo_b, has_hi_s, has_lo_s)
    came = (has_lo_b, has_hi_b, has_lo_s, has_hi_s)
    peer = (hi_b, lo_b, hi_s, lo_s)

    own = pl.ds(O, CY)

    barrier = pltpu.get_barrier_semaphore()

    def around(axis, me, n, distance, sem):
        for to in (lax.rem(me + distance, n), lax.rem(me + n - distance, n)):
            pl.semaphore_signal(sem, inc=1, device_id={axis: to}, device_id_type=MESH)

    around("blk", mb, nb, 1, barrier)
    around("span", ms, nsp, 1, barrier)

    def rounds(n):
        return max(0, (n // 2 - 1).bit_length())

    def greet(j):
        if j < rounds(nb):
            around("blk", mb, nb, 2**j, gb.at[j])
        if j < rounds(nsp):
            around("span", ms, nsp, 2**j, gs.at[j])

    def heard(j):
        if j < rounds(nb):
            pl.semaphore_wait(gb.at[j], 2)
        if j < rounds(nsp):
            pl.semaphore_wait(gs.at[j], 2)

    def far_first(k, n):
        step = (k + 1) // 2
        return n // 2 + jnp.where(lax.rem(k, 2) == 1, step, -step)

    loads = [
        pltpu.make_async_copy(adj_in, adj.at[0, :, pl.ds(1, CX), own, :], lsem.at[0]),
        pltpu.make_async_copy(vel_in, vel, lsem.at[1]),
        pltpu.make_async_copy(src_in, src, lsem.at[2]),
        pltpu.make_async_copy(con_in, con.at[pl.ds(1, CH), own, :], lsem.at[3]),
        pltpu.make_async_copy(tem_in, tem.at[0, pl.ds(1, CH), own, :], lsem.at[4]),
        pltpu.make_async_copy(heat_in, heat, lsem.at[5]),
        pltpu.make_async_copy(wall_in.at[0], wall, lsem.at[6]),
        pltpu.make_async_copy(dif_in, dif, lsem.at[7]),
        pltpu.make_async_copy(jac_in, jac, lsem.at[8]),
        pltpu.make_async_copy(owner_in, owner_v, lsem.at[9]),
        pltpu.make_async_copy(target_in, target_v, lsem.at[10]),
    ]
    for copy in loads:
        copy.start()

    def zero_halos(cond, put):
        @pl.when(jnp.logical_not(cond))
        def _():
            put()

    def z_lo_b():
        for e in range(SWEEPS):
            adj[e, :, 0, O : O + CY, :] = jnp.zeros((NF, CY, NZ), F32)
            tem[e, 0, O : O + CY, :] = jnp.zeros((CY, NZ), F32)
        con[0, O : O + CY, :] = jnp.zeros((CY, NZ), F32)
        dlow[...] = jnp.zeros_like(dlow)

    def z_hi_b():
        for e in range(SWEEPS):
            adj[e, :, CX + 1, O : O + CY, :] = jnp.zeros((NF, CY, NZ), F32)
            tem[e, CH + 1, O : O + CY, :] = jnp.zeros((CY, NZ), F32)
        con[CH + 1, O : O + CY, :] = jnp.zeros((CY, NZ), F32)
        kc[5:9, O - W4 : O + CY + W4, :] = jnp.zeros((4, CY + 2 * W4, NZ), F32)
        r0_up[...] = jnp.zeros_like(r0_up)

    def z_span(halo, wide):
        def put():
            for e in range(SWEEPS):
                adj[e, :, 1 : CX + 1, halo : halo + 1, :] = jnp.zeros((NF, CX, 1, NZ), F32)
                tem[e, 1 : CH + 1, halo : halo + 1, :] = jnp.zeros((CH, 1, NZ), F32)
            con[1 : CH + 1, wide : wide + W4, :] = jnp.zeros((CH, W4, NZ), F32)
            hc[4, wide : wide + W4, :] = jnp.zeros((W4, NZ), F32)

        return put

    zero_halos(has_lo_b, z_lo_b)
    zero_halos(has_hi_b, z_hi_b)
    zero_halos(has_lo_s, z_span(O - 1, O - W4))
    zero_halos(has_hi_s, z_span(O + CY, O + CY))

    pl.semaphore_wait(barrier, 4)
    greet(0)

    def fluid_copy(e, d, first=False):
        if d < 2:
            plane = (CX, 1)[d]
            fields = pl.ds(0, NF - 1 if (e, d) == (SWEEPS - 1, 0) else NF)
            source = adj_in.at[:, plane - 1] if first else adj.at[e, fields, plane, own, :]
            dest = adj.at[e, fields, (0, CX + 1)[d], own, :]
        else:
            row = (CY - 1, 0)[d - 2]
            planes = pl.ds(2, CX - 1) if e == SWEEPS - 1 else pl.ds(1, CX)
            source = (
                adj_in.at[:, :, pl.ds(row, 1), :]
                if first
                else adj.at[e, :, planes, pl.ds(O + row, 1), :]
            )
            dest = adj.at[e, :, planes, pl.ds((O - 1, O + CY)[d - 2], 1), :]
        return pltpu.make_async_remote_copy(
            source, dest, fs.at[e, d], fr.at[e, d], device_id=peer[d], device_id_type=MESH
        )

    def early_copy(d):
        e = SWEEPS - 1
        if d == 0:
            source = adj.at[e, NF - 1, CX, own, :]
            dest = adj.at[e, NF - 1, 0, own, :]
        else:
            source = adj.at[e, :, 1, pl.ds(O + (CY - 1, 0)[d - 2], 1), :]
            dest = adj.at[e, :, 1, pl.ds((O - 1, O + CY)[d - 2], 1), :]
        i = max(0, d - 1)
        return pltpu.make_async_remote_copy(
            source, dest, ws.at[i], wr.at[i], device_id=peer[d], device_id_type=MESH
        )

    def solid_copy(e, d, first=False):
        if d < 2:
            plane = (CH, 1)[d]
            source = tem_in.at[plane - 1] if first else tem.at[e, plane, own, :]
            dest = tem.at[e, (0, CH + 1)[d], own, :]
        else:
            row = (CY - 1, 0)[d - 2]
            source = (
                tem_in.at[:, pl.ds(row, 1), :]
                if first
                else tem.at[e, pl.ds(1, CH), pl.ds(O + row, 1), :]
            )
            dest = tem.at[e, pl.ds(1, CH), pl.ds((O - 1, O + CY)[d - 2], 1), :]
        return pltpu.make_async_remote_copy(
            source, dest, ts.at[e, d], tr.at[e, d], device_id=peer[d], device_id_type=MESH
        )

    def con_copy(d):
        if d < 2:
            source = con_in.at[(CH - 1, 0)[d]]
            dest = con.at[(0, CH + 1)[d], own, :]
        else:
            source = con_in.at[:, pl.ds((CY - W4, 0)[d - 2], W4), :]
            dest = con.at[pl.ds(1, CH), pl.ds((O - W4, O + CY)[d - 2], W4), :]
        return pltpu.make_async_remote_copy(
            source, dest, ks.at[d], kr.at[d], device_id=peer[d], device_id_type=MESH
        )

    wide_rows = pl.ds(O - W4, CY + 2 * W4)
    wide_copy = pltpu.make_async_remote_copy(
        con.at[pl.ds(1, 4), wide_rows, :],
        kc.at[pl.ds(5, 4), wide_rows, :],
        ks.at[4],
        kr.at[4],
        device_id=lo_b,
        device_id_type=MESH,
    )
    r0_copy = pltpu.make_async_remote_copy(
        r0.at[pl.ds(0, 3)], r0_up, ks.at[5], kr.at[5], device_id=lo_b, device_id_type=MESH
    )
    dl_copy = pltpu.make_async_remote_copy(
        dup, dlow, ks.at[6], kr.at[6], device_id=hi_b, device_id_type=MESH
    )

    def edge_copy(d):
        source = hc.at[4, pl.ds((O + CY - W4, O)[d - 2], W4), :]
        dest = hc.at[4, pl.ds((O - W4, O + CY)[d - 2], W4), :]
        return pltpu.make_async_remote_copy(
            source, dest, ks.at[5 + d], kr.at[5 + d], device_id=peer[d], device_id_type=MESH
        )

    def go(cond, copy):
        @pl.when(cond)
        def _():
            copy.start()

    def arrived(cond, copy):
        @pl.when(cond)
        def _():
            copy.wait_recv()

    def left(cond, copy):
        @pl.when(cond)
        def _():
            copy.wait_send()

    def spread(send, recv, sem):
        @pl.loop(0, nb - 1)
        def _(k):
            to = lax.rem(mb + far_first(k, nb), nb)
            pltpu.make_async_remote_copy(
                send.at[pl.ds(to * slot, slot), :],
                recv.at[pl.ds(mb * slot, slot), :],
                as_.at[sem],
                ar.at[sem],
                device_id={"blk": to},
                device_id_type=MESH,
            ).start()

    def spread_waiter(send, recv, sem):
        rows = pl.ds(0, (nb - 1) * slot)
        return pltpu.make_async_remote_copy(
            send.at[rows, :], recv.at[rows, :], as_.at[sem], ar.at[sem], device_id=hi_b, device_id_type=MESH
        )

    for d in range(4):
        go(has[d], fluid_copy(0, d, True))
    for d in range(4):
        go(has[d], con_copy(d))
    for d in range(4):
        go(has[d], solid_copy(0, d, True))

    own_block = pl.ds(mb * slot, slot)
    loads[9].wait()
    loads[10].wait()
    ow = owner_v[...].astype(F32)
    tg = target_v[...].astype(F32)
    rows2 = lax.broadcasted_iota(jnp.int32, (CY, CY), 0)
    cols2 = lax.broadcasted_iota(jnp.int32, (CY, CY), 1)
    ow_l = jnp.broadcast_to(ow, (CY, CY))
    ow_s = jnp.sum(jnp.where(rows2 == cols2, ow_l, 0.0), axis=1, keepdims=True)
    same = jnp.where(jnp.broadcast_to(ow_s, (CY, CY)) == ow_l, 1.0, 0.0)
    rank_l = jnp.sum(jnp.where(rows2 < cols2, same, 0.0), axis=0, keepdims=True)
    rank_s = jnp.sum(jnp.where(cols2 < rows2, same, 0.0), axis=1, keepdims=True)
    slot_l = ow * float(slot) + rank_l
    slot_s = ow_s * float(slot) + rank_s
    p_rows = lax.broadcasted_iota(jnp.int32, (ns, CY), 0).astype(F32)
    hot = jnp.broadcast_to(slot_l, (ns, CY)) == p_rows
    pmat[...] = jnp.where(hot, 1.0, 0.0).astype(jnp.bfloat16)
    p_cols = lax.broadcasted_iota(jnp.int32, (CY, ns), 1).astype(F32)
    pmat_t[...] = jnp.where(jnp.broadcast_to(slot_s, (CY, ns)) == p_cols, 1.0, 0.0).astype(jnp.bfloat16)
    meta = jnp.sum(jnp.where(hot, jnp.broadcast_to(tg + 1.0, (ns, CY)), 0.0), axis=1, keepdims=True) - 1.0
    msend[...] = jnp.broadcast_to(meta, (ns, NZ))
    mrecv[own_block, :] = msend[own_block, :]

    lane = lax.broadcasted_iota(jnp.int32, (CY, NZ), 1)
    first_lane, last_lane = lane == 0, lane == NZ - 1

    loads[1].wait()
    loads[7].wait()
    loads[8].wait()

    @pl.loop(0, CX)
    def _(x):
        total = vel[0, x] + vel[1, x] + vel[2, x]
        for f in range(NF):
            inv[f, x] = OMEGA / (total + (6.0 * dif[f] + jac[f, f]))

    for k in range(3):
        dl[k] = jnp.zeros((9, ROWS, NZ), F32)
    for p in range(9):
        if p != 4:
            hc[p] = jnp.zeros((ROWS, NZ), F32)
        kc[p, 0 : O - W4, :] = jnp.zeros((O - W4, NZ), F32)
        kc[p, O + CY + W4 : ROWS, :] = jnp.zeros((ROWS - O - CY - W4, NZ), F32)
    hc[4, 0 : O - W4, :] = jnp.zeros((O - W4, NZ), F32)
    hc[4, O + CY + W4 : ROWS, :] = jnp.zeros((ROWS - O - CY - W4, NZ), F32)

    def fluid_plane(e, x, fields=range(NF)):
        centre = [adj[e, f, x, O : O + CY, :] for f in range(NF)]
        u = [vel[i, x - 1] for i in range(3)]
        total = u[0] + u[1] + u[2]
        residuals = []
        for f in fields:
            c, d = centre[f], dif[f]
            x_next = adj[e, f, x + 1, O : O + CY, :]
            y_next = adj[e, f, x, O + 1 : O + 1 + CY, :]
            z_next = jnp.where(last_lane, 0.0, pltpu.roll(c, NZ - 1, 1))
            back = (
                adj[e, f, x - 1, O : O + CY, :]
                + adj[e, f, x, O - 1 : O - 1 + CY, :]
                + jnp.where(first_lane, 0.0, pltpu.roll(c, 1, 1))
            )
            residual = src[f, x - 1] - (6.0 * d + total) * c + d * back
            residual = residual + (d + u[0]) * x_next + (d + u[1]) * y_next + (d + u[2]) * z_next
            mixing = jac[f, 0] * centre[0]
            for g in range(1, NF):
                mixing = mixing + jac[f, g] * centre[g]
            residual = residual - mixing
            adj[e + 1, f, x, O : O + CY, :] = c + inv[f, x - 1] * residual
            residuals.append(residual)
        return residuals

    def select(matrix, values):
        total = None
        for _ in range(3):
            part = values.astype(jnp.bfloat16)
            values = values - part.astype(F32)
            term = jnp.dot(matrix, part, preferred_element_type=F32)
            total = term if total is None else total + term
        return total

    def folded(values):
        return (values * values).reshape(CY // 8, 8, NZ).sum(axis=0)

    def flows2(q, k, gz, i, a, n):
        c, kk = q[i, pl.ds(a, n), :], k[i, pl.ds(a, n), :]
        flow = (kk + k[i + 1, pl.ds(a, n), :]) * q[i + 1, pl.ds(a, n), :]
        flow = flow + (kk + k[i - 1, pl.ds(a, n), :]) * q[i - 1, pl.ds(a, n), :]
        flow = flow + (kk + k[i, pl.ds(a + 1, n), :]) * q[i, pl.ds(a + 1, n), :]
        flow = flow + (kk + k[i, pl.ds(a - 1, n), :]) * q[i, pl.ds(a - 1, n), :]
        flow = flow + gz * pltpu.roll(c, NZ - 1, 1) + pltpu.roll(gz * c, 1, 1)
        return c, flow

    def coefficients(k, i, a, n):
        kk = k[i, pl.ds(a, n), :]
        at = lax.broadcasted_iota(jnp.int32, (n, NZ), 1)
        k_next = jnp.where(at == NZ - 1, 0.0, pltpu.roll(kk, NZ - 1, 1))
        k_back = jnp.where(at == 0, 0.0, pltpu.roll(kk, 1, 1))
        diagonal = 6.0 * kk + k[i + 1, pl.ds(a, n), :] + k[i - 1, pl.ds(a, n), :]
        diagonal = diagonal + k[i, pl.ds(a + 1, n), :] + k[i, pl.ds(a - 1, n), :] + k_next + k_back
        gz = jnp.where(at == NZ - 1, 0.0, kk + k_next)
        return gz, diagonal

    def solid_plane(e, p):
        c, flow = flows2(tem.at[e], con, sgz[p - 1], p, O, CY)
        residual = heat[p - 1] - 0.5 * (sd2[p - 1] * c - flow)
        return residual, c + sdi[p - 1] * residual

    def solid_prepare():
        loads[3].wait()
        for d in range(4):
            arrived(came[d], con_copy(d))

        @pl.loop(1, CH + 1)
        def _(p):
            gz, diagonal = coefficients(con, p, O, CY)
            sgz[p - 1] = gz
            sd2[p - 1] = diagonal
            sdi[p - 1] = (2.0 * OMEGA) / diagonal

    def solid_wait(e):
        for d in range(4):
            arrived(came[d], solid_copy(e, d, e == 0))

    def solid_sweep(e):
        def put(p):
            tem[e + 1, p, O : O + CY, :] = solid_plane(e, p)[1]

        put(1)
        put(CH)
        for d in range(2):
            go(has[d], solid_copy(e + 1, d))

        @pl.loop(2, CH)
        def _(p):
            put(p)

        for d in range(2, 4):
            go(has[d], solid_copy(e + 1, d))

    loads[0].wait()
    loads[2].wait()
    for e in range(SWEEPS - 1):
        for d in range(4):
            arrived(came[d], fluid_copy(e, d, e == 0))
        split = e == SWEEPS - 2
        fluid_plane(e, CX)
        if split:
            go(has[0], early_copy(0))
        go(has[0], fluid_copy(e + 1, 0))
        fluid_plane(e, 1)
        if split:
            for d in (2, 3):
                go(has[d], early_copy(d))
        go(has[1], fluid_copy(e + 1, 1))

        if e == 0:
            heard(0)
            greet(1)

        @pl.loop(2, CX)
        def _(x):
            fluid_plane(e, x)

        for d in range(2, 4):
            go(has[d], fluid_copy(e + 1, d))
        if e == 0:
            solid_prepare()
            loads[4].wait()
            loads[5].wait()
        if e == 1:
            heard(2)
            greet(3)
        solid_wait(e)
        solid_sweep(e)
        if e == 0:
            heard(1)
            greet(2)
        if e == 1:
            heard(3)
            spread(msend, mrecv, 0)
        if e == SWEEPS - 2:
            go(has_lo_b, wide_copy)

    n40 = CY + 2 * W4
    for p in range(5):
        kc[p, O - W4 : O + CY + W4, :] = con[12 + p, O - W4 : O + CY + W4, :]

    loads[6].wait()

    e = SWEEPS - 1
    for d in (0, 2, 3):
        arrived(came[d], early_copy(d))
    fluid_plane(e, 1, (NF - 1,))
    flux = wall[...] * adj[SWEEPS, NF - 1, 1, O : O + CY, :]
    fsend[...] = select(pmat[...], flux)
    spread(fsend, frecv, 1)
    frecv[own_block, :] = fsend[own_block, :]

    for d in range(4):
        arrived(came[d], fluid_copy(e, d))

    def more(x, carry):
        return tuple(a + folded(r) for a, r in zip(carry, fluid_plane(e, x)))

    zero8 = jnp.zeros((8, NZ), F32)
    squares = lax.fori_loop(1, CX + 1, more, (zero8,) * NF)
    outs = [
        pltpu.make_async_copy(
            adj.at[SWEEPS, pl.ds(0, NF - 1), pl.ds(1, CX), own, :], adj_out.at[pl.ds(0, NF - 1)], osem.at[0]
        ),
        pltpu.make_async_copy(
            adj.at[SWEEPS, NF - 1, pl.ds(2, CX - 1), own, :], adj_out.at[NF - 1, pl.ds(1, CX - 1)], osem.at[1]
        ),
    ]
    for copy in outs:
        copy.start()

    solid_wait(e)

    def edge(first, count, at):
        def body(i, carry):
            residual, new = solid_plane(e, first + i)
            tout[first + i - 1] = new
            r0[at + i] = residual
            return carry + folded(residual)

        return lax.fori_loop(0, count, body, zero8)

    low_squares = edge(1, 3, 0)
    go(has_lo_b, r0_copy)
    edge(13, 4, 3)

    def middle(p, carry):
        residual, new = solid_plane(e, p)
        tout[p - 1] = new
        return carry + folded(residual)

    solid_squares = lax.fori_loop(4, 13, middle, zero8)
    outs.append(pltpu.make_async_copy(tout.at[pl.ds(3, 9)], sol_out.at[pl.ds(3, 9)], osem.at[2]))
    outs[-1].start()
    solid_squares = solid_squares + jnp.where(has_lo_b, 0.0, low_squares)

    arrived(has_hi_b, wide_copy)
    row = lax.broadcasted_iota(jnp.int32, (n40, NZ), 0) - W4
    inside = (row >= jnp.where(has_lo_s, -3, 0)) & (row <= jnp.where(has_hi_s, CY + 2, CY - 1))

    @pl.loop(1, 8)
    def _(i):
        gz, diagonal = coefficients(kc, i, O - W4, n40)
        ok = inside & ((i < 5) | has_hi_b)
        cgz[i] = gz
        cd2[i] = diagonal
        cdi[i] = jnp.where(ok, (2.0 * OMEGA) / jnp.where(ok, diagonal, 1.0), 0.0)

    lane8 = lax.broadcasted_iota(jnp.int32, (8, NZ), 1)
    row8 = lax.broadcasted_iota(jnp.int32, (8, NZ), 0)
    sums = jnp.zeros((8, NZ), F32)
    for f in range(NF):
        sums = sums + jnp.where(row8 == f, jnp.broadcast_to(jnp.sum(squares[f], axis=0, keepdims=True), (8, NZ)), 0.0)

    spread_waiter(msend, mrecv, 0).wait_recv()
    hit = jnp.where(
        mrecv[...] == lax.broadcasted_iota(jnp.int32, (ns, NZ), 1).astype(F32), 1.0, 0.0
    )
    smat_t[...] = hit.astype(jnp.bfloat16)
    smat[...] = jnp.transpose(hit).astype(jnp.bfloat16)

    spread_waiter(fsend, frecv, 1).wait_recv()
    hc[4, O : O + CY, :] = select(smat[0:CY, :], frecv[...])
    for d in (2, 3):
        go(has[d], edge_copy(d))
    for d in (2, 3):
        arrived(came[d], edge_copy(d))
    arrived(has_hi_b, r0_copy)

    wide = slice(O - W4, O + CY + W4)
    dl[0, 4, wide, :] = cdi[4] * hc[4, wide, :]
    for k in range(2):

        @pl.loop(3 - k, 6 + k)
        def _(i):
            c, flow = flows2(dl.at[k], kc, cgz[i], i, O - W4, n40)
            dl[k + 1, i, wide, :] = c + cdi[i] * (hc[i, wide, :] - 0.5 * (cd2[i] * c - flow))

    mid = pl.ds(W4, CY)

    def last(i):
        c, flow = flows2(dl.at[2], kc, cgz[i, mid, :], i, O, CY)
        residual = hc[i, O : O + CY, :] - 0.5 * (cd2[i, mid, :] * c - flow)
        return residual, c + cdi[i, mid, :] * residual

    def last_own(i, carry):
        residual, delta = last(i)
        tout[11 + i] = tout[11 + i] + delta
        return carry + folded(residual + r0[2 + i])

    solid_squares = lax.fori_loop(1, 5, last_own, solid_squares)

    def last_up(i, carry):
        residual, delta = last(i)
        dup[i - 5] = delta
        return carry + folded(residual + r0_up[i - 5])

    up_squares = lax.fori_loop(5, 8, last_up, zero8)
    go(has_hi_b, dl_copy)
    solid_squares = solid_squares + jnp.where(has_hi_b, up_squares, 0.0)
    sums = sums + jnp.where(row8 == NF, jnp.broadcast_to(jnp.sum(solid_squares, axis=0, keepdims=True), (8, NZ)), 0.0)
    totals = jnp.broadcast_to(jnp.sum(sums, axis=1, keepdims=True), (8, NZ))
    totals = jnp.sum(jnp.where(row8 == lane8, totals, 0.0), axis=0, keepdims=True)

    back = select(smat_t[:, 0:CY], tout[CH - 1])
    free = lax.rem(lax.broadcasted_iota(jnp.int32, (ns, NZ), 0), slot) == slot - 1
    rsend[...] = jnp.where(free, jnp.broadcast_to(totals, (ns, NZ)), back)
    spread(rsend, rrecv, 2)
    rrecv[own_block, :] = rsend[own_block, :]
    outs.append(pltpu.make_async_copy(tout.at[pl.ds(12, 4)], sol_out.at[pl.ds(12, 4)], osem.at[3]))
    outs[-1].start()

    arrived(has_lo_b, dl_copy)
    for i in range(3):
        tout[i] = tout[i] + dlow[i]
    outs.append(pltpu.make_async_copy(tout.at[pl.ds(0, 3)], sol_out.at[pl.ds(0, 3)], osem.at[4]))
    outs[-1].start()

    spread_waiter(rsend, rrecv, 2).wait_recv()
    got = rrecv[...]
    nsend[...] = jnp.sum(jnp.where(free, got, 0.0), axis=0, keepdims=True)

    def norm_copy(to):
        return pltpu.make_async_remote_copy(
            nsend, nrecv.at[ms], as_.at[3], ar.at[3], device_id={"span": to}, device_id_type=MESH
        )

    @pl.loop(1, nsp)
    def _(k):
        norm_copy(lax.rem(ms + k, nsp)).start()

    nrecv[ms] = nsend[...]
    returned = select(pmat_t[...], got)
    fin[...] = adj[SWEEPS, NF - 1, 1, O : O + CY, :] + wall[...] * returned
    outs.append(pltpu.make_async_copy(fin, adj_out.at[NF - 1, 0], osem.at[5]))
    outs[-1].start()

    norm_waiter = pltpu.make_async_remote_copy(
        nrecv.at[pl.ds(0, nsp - 1)],
        nrecv.at[pl.ds(0, nsp - 1)],
        as_.at[3],
        ar.at[3],
        device_id=hi_s,
        device_id_type=MESH,
    )
    norm_waiter.wait_recv()
    total = nrecv[0]
    for k in range(1, nsp):
        total = total + nrecv[k]
    cells = jnp.where(lane8 < NF, fluid_cells, solid_cells)
    norm_out[...] = jnp.sqrt(jnp.broadcast_to(total, (8, NZ)) / cells)

    for e in range(SWEEPS):
        for d in range(4):
            left(has[d], fluid_copy(e, d, e == 0))
            left(has[d], solid_copy(e, d, e == 0))
    for d in range(4):
        left(has[d], con_copy(d))
    for d in (0, 2, 3):
        left(has[d], early_copy(d))
    left(has_lo_b, wide_copy)
    left(has_lo_b, r0_copy)
    left(has_hi_b, dl_copy)
    for d in (2, 3):
        left(has[d], edge_copy(d))
    spread_waiter(msend, mrecv, 0).wait_send()
    spread_waiter(fsend, frecv, 1).wait_send()
    spread_waiter(rsend, rrecv, 2).wait_send()
    norm_waiter.wait_send()
    for copy in outs:
        copy.wait()


def shards(
    nb,
    nsp,
    slot,
    fluid_adjoint_in,
    fluid_source,
    velocity,
    diffusion,
    jacobian,
    wall_coefficient,
    metal_costate_prior,
    solid_source,
    conductivity,
    tile_owner,
    tile_target,
):
    ns = nb * slot
    every = nb * nsp

    def stay(x):
        return pltpu.with_memory_space_constraint(x, pltpu.HBM)

    anywhere = pl.BlockSpec(memory_space=pl.ANY)
    vmem = pl.BlockSpec(memory_space=pltpu.VMEM)
    V = pltpu.VMEM
    n40 = CY + 2 * W4
    dma = pltpu.SemaphoreType.DMA
    scratch = [
        pltpu.SMEM((NF,), F32),
        pltpu.SMEM((NF, NF), F32),
        V((1, CY), jnp.int32),
        V((1, CY), jnp.int32),
        V((SWEEPS + 1, NF, CX + 2, ROWS, NZ), F32),
        V((NF, CX, CY, NZ), F32),
        V((3, CX, CY, NZ), F32),
        V((NF, CX, CY, NZ), F32),
        V((CY, NZ), F32),
        V((CY, NZ), F32),
        V((SWEEPS, CH + 2, ROWS, NZ), F32),
        V((CH + 2, ROWS, NZ), F32),
        V((CH, CY, NZ), F32),
        V((CH, CY, NZ), F32),
        V((CH, CY, NZ), F32),
        V((CH, CY, NZ), F32),
        V((CH, CY, NZ), F32),
        V((7, CY, NZ), F32),
        V((3, CY, NZ), F32),
        V((9, ROWS, NZ), F32),
        V((8, n40, NZ), F32),
        V((8, n40, NZ), F32),
        V((8, n40, NZ), F32),
        V((9, ROWS, NZ), F32),
        V((3, 9, ROWS, NZ), F32),
        V((3, CY, NZ), F32),
        V((3, CY, NZ), F32),
        V((ns, CY), jnp.bfloat16),
        V((CY, ns), jnp.bfloat16),
        V((NZ, ns), jnp.bfloat16),
        V((ns, NZ), jnp.bfloat16),
    ]
    scratch += [V((ns, NZ), F32)] * 6
    scratch += [V((1, NZ), F32), V((nsp, 1, NZ), F32)]
    scratch += [
        dma((11,)),
        dma((6,)),
        dma((SWEEPS, 4)),
        dma((SWEEPS, 4)),
        dma((SWEEPS, 4)),
        dma((SWEEPS, 4)),
        dma((9,)),
        dma((9,)),
        dma((1,)),
        dma((1,)),
        dma((4,)),
        dma((4,)),
        dma((3,)),
        dma((3,)),
        pltpu.SemaphoreType.REGULAR((8,)),
        pltpu.SemaphoreType.REGULAR((8,)),
    ]
    adjoint, solid, norms = pl.pallas_call(
        functools.partial(
            kernel, nb, nsp, slot, float(CX * CY * NZ * every), float(CH * CY * NZ * every)
        ),
        out_shape=(
            jax.ShapeDtypeStruct(fluid_adjoint_in.shape, F32),
            jax.ShapeDtypeStruct(metal_costate_prior.shape, F32),
            jax.ShapeDtypeStruct((8, NZ), F32),
        ),
        in_specs=[anywhere] * 11,
        out_specs=(anywhere, anywhere, vmem),
        scratch_shapes=scratch,
        compiler_params=pltpu.CompilerParams(collective_id=0, has_side_effects=True, vmem_limit_bytes=24 * 2**20),
        name="iteration",
    )(
        *map(
            stay,
            (
                fluid_adjoint_in,
                fluid_source,
                velocity,
                diffusion,
                jacobian,
                wall_coefficient,
                metal_costate_prior,
                solid_source,
                conductivity,
                tile_owner.reshape(1, CY),
                tile_target,
            ),
        )
    )
    return adjoint, solid, norms[0, : NF + 1]


def solution(mesh, slot=4):
    placed = (
        P(None, "blk", "span", None),
        P(None, "blk", "span", None),
        P(None, "blk", "span", None),
        P(),
        P(),
        P("blk", "span", None),
        P("blk", "span", None),
        P("blk", "span", None),
        P("blk", "span", None),
        P("span", "blk", None),
        P("span", "blk"),
    )
    return jax.shard_map(
        functools.partial(shards, mesh.shape["blk"], mesh.shape["span"], slot),
        mesh=mesh,
        in_specs=placed,
        out_specs=(P(None, "blk", "span", None), P("blk", "span", None), P()),
        check_vma=False,
    )
```

```python
import functools

import jax
import jax.numpy as jnp
from jax import lax
from jax.experimental import pallas as pl
from jax.experimental.pallas import tpu as pltpu
from jax.sharding import PartitionSpec as P

MESH = pl.DeviceIdType.MESH
F32 = jnp.float32
NF = 5
CX = 8
CY = 32
CH = 16
NZ = 128
ROWS = 48
O = 8
W4 = 4
SWEEPS = 4
OMEGA = 0.8
GROUPS = ((4, 1), (2, 2), (0, 2))


def kernel(
    nb,
    nsp,
    slot,
    fluid_cells,
    solid_cells,
    adj_in,
    src_in,
    vel_in,
    dif_in,
    jac_in,
    wall_in,
    tem_in,
    heat_in,
    con_in,
    owner_in,
    target_in,
    adj_out,
    sol_out,
    norm_out,
    dif,
    jac,
    owner_v,
    target_v,
    adj,
    src,
    vel,
    inv,
    wall,
    fin,
    tem,
    con,
    heat,
    sgz,
    sd2,
    sdi,
    tout,
    r0,
    r0_up,
    kc,
    cgz,
    cd2,
    cdi,
    hc,
    dl,
    dup,
    dlow,
    pmat,
    pmat_t,
    smat,
    smat_t,
    msend,
    mrecv,
    fsend,
    frecv,
    rsend,
    rrecv,
    nmine,
    nrow,
    nsend,
    nrecv,
    lsem,
    osem,
    xfs,
    xfr,
    yfs,
    ybr,
    yir,
    ts,
    tr,
    ks,
    kr,
    xs,
    xr,
    as_,
    ar,
    gb,
    gs,
):
    ns = nb * slot
    mb = lax.axis_index("blk")
    ms = lax.axis_index("span")
    has_lo_b, has_hi_b = mb > 0, mb < nb - 1
    has_lo_s, has_hi_s = ms > 0, ms < nsp - 1
    lo_b, hi_b = {"blk": mb - 1}, {"blk": mb + 1}
    lo_s, hi_s = {"span": ms - 1}, {"span": ms + 1}
    has = (has_hi_b, has_lo_b, has_hi_s, has_lo_s)
    came = (has_lo_b, has_hi_b, has_lo_s, has_hi_s)
    peer = (hi_b, lo_b, hi_s, lo_s)

    own = pl.ds(O, CY)

    frecv[...] = jnp.zeros_like(frecv)
    rrecv[...] = jnp.zeros_like(rrecv)

    barrier = pltpu.get_barrier_semaphore()

    def around(axis, me, n, distance, sem):
        for to in (lax.rem(me + distance, n), lax.rem(me + n - distance, n)):
            pl.semaphore_signal(sem, inc=1, device_id={axis: to}, device_id_type=MESH)

    around("blk", mb, nb, 1, barrier)
    around("span", ms, nsp, 1, barrier)

    def rounds(n):
        return max(0, (n // 2 - 1).bit_length())

    def greet(j):
        if j < rounds(nb):
            around("blk", mb, nb, 2**j, gb.at[j])
        if j < rounds(nsp):
            around("span", ms, nsp, 2**j, gs.at[j])

    def heard(j):
        if j < rounds(nb):
            pl.semaphore_wait(gb.at[j], 2)
        if j < rounds(nsp):
            pl.semaphore_wait(gs.at[j], 2)

    loads = [
        pltpu.make_async_copy(adj_in, adj.at[0, :, pl.ds(1, CX), own, :], lsem.at[0]),
        pltpu.make_async_copy(vel_in, vel, lsem.at[1]),
        pltpu.make_async_copy(src_in, src, lsem.at[2]),
        pltpu.make_async_copy(con_in, con.at[pl.ds(1, CH), own, :], lsem.at[3]),
        pltpu.make_async_copy(tem_in, tem.at[0, pl.ds(1, CH), own, :], lsem.at[4]),
        pltpu.make_async_copy(heat_in, heat, lsem.at[5]),
        pltpu.make_async_copy(wall_in.at[0], wall, lsem.at[6]),
        pltpu.make_async_copy(dif_in, dif, lsem.at[7]),
        pltpu.make_async_copy(jac_in, jac, lsem.at[8]),
        pltpu.make_async_copy(owner_in, owner_v, lsem.at[9]),
        pltpu.make_async_copy(target_in, target_v, lsem.at[10]),
    ]
    for copy in loads:
        copy.start()

    def zero_halos(cond, put):
        @pl.when(jnp.logical_not(cond))
        def _():
            put()

    def z_lo_b():
        for e in range(SWEEPS):
            adj[e, :, 0, O : O + CY, :] = jnp.zeros((NF, CY, NZ), F32)
            tem[e, 0, O : O + CY, :] = jnp.zeros((CY, NZ), F32)
        con[0, O : O + CY, :] = jnp.zeros((CY, NZ), F32)
        dlow[...] = jnp.zeros_like(dlow)

    def z_hi_b():
        for e in range(SWEEPS):
            adj[e, :, CX + 1, O : O + CY, :] = jnp.zeros((NF, CY, NZ), F32)
            tem[e, CH + 1, O : O + CY, :] = jnp.zeros((CY, NZ), F32)
        con[CH + 1, O : O + CY, :] = jnp.zeros((CY, NZ), F32)
        kc[5:9, O - W4 : O + CY + W4, :] = jnp.zeros((4, CY + 2 * W4, NZ), F32)
        r0_up[...] = jnp.zeros_like(r0_up)

    def z_span(halo, wide):
        def put():
            for e in range(SWEEPS):
                adj[e, :, 1 : CX + 1, halo : halo + 1, :] = jnp.zeros((NF, CX, 1, NZ), F32)
                tem[e, 1 : CH + 1, halo : halo + 1, :] = jnp.zeros((CH, 1, NZ), F32)
            con[1 : CH + 1, wide : wide + W4, :] = jnp.zeros((CH, W4, NZ), F32)
            hc[4, wide : wide + W4, :] = jnp.zeros((W4, NZ), F32)

        return put

    zero_halos(has_lo_b, z_lo_b)
    zero_halos(has_hi_b, z_hi_b)
    zero_halos(has_lo_s, z_span(O - 1, O - W4))
    zero_halos(has_hi_s, z_span(O + CY, O + CY))

    pl.semaphore_wait(barrier, 4)
    greet(0)

    share = (CX - 2) // len(GROUPS)

    def x_copy(e, d, g):
        plane, fields = (CX, 1)[d], pl.ds(*GROUPS[g])
        return pltpu.make_async_remote_copy(
            adj_in.at[fields, plane - 1] if e == 0 else adj.at[e, fields, plane, own, :],
            adj.at[e, fields, (0, CX + 1)[d], own, :],
            xfs.at[d],
            xfr.at[e, d, g],
            device_id=peer[d],
            device_id_type=MESH,
        )

    def y_copy(e, d, fields, planes, sem):
        row, halo = (CY - 1, 0)[d - 2], (O - 1, O + CY)[d - 2]
        inner = pl.ds(planes.start - 1, planes.size)
        return pltpu.make_async_remote_copy(
            adj_in.at[fields, inner, pl.ds(row, 1), :]
            if e == 0
            else adj.at[e, fields, planes, pl.ds(O + row, 1), :],
            adj.at[e, fields, planes, pl.ds(halo, 1), :],
            yfs.at[d - 2],
            sem,
            device_id=peer[d],
            device_id_type=MESH,
        )

    def outer_copy(e, d, g, x, count=1):
        return y_copy(e, d, pl.ds(*GROUPS[g]), pl.ds(x, count), ybr.at[e, d - 2, g])

    def inner_copy(e, d, g):
        return y_copy(e, d, pl.ds(0, NF), pl.ds(2 + share * g, share), yir.at[e, d - 2, g])

    def fluid_sent(d):
        ref = src.at[:, pl.ds(0, SWEEPS)] if d < 2 else src.at[:, 0]
        return pltpu.make_async_remote_copy(
            ref, ref, xfs.at[d] if d < 2 else yfs.at[d - 2], xfr.at[0, 0, 0], device_id=peer[d], device_id_type=MESH
        )

    def solid_copy(e, d, first=False):
        if d < 2:
            plane = (CH, 1)[d]
            source = tem_in.at[plane - 1] if first else tem.at[e, plane, own, :]
            dest = tem.at[e, (0, CH + 1)[d], own, :]
        else:
            row = (CY - 1, 0)[d - 2]
            source = (
                tem_in.at[:, pl.ds(row, 1), :]
                if first
                else tem.at[e, pl.ds(1, CH), pl.ds(O + row, 1), :]
            )
            dest = tem.at[e, pl.ds(1, CH), pl.ds((O - 1, O + CY)[d - 2], 1), :]
        return pltpu.make_async_remote_copy(
            source, dest, ts.at[e, d], tr.at[e, d], device_id=peer[d], device_id_type=MESH
        )

    def con_copy(d):
        if d < 2:
            source = con_in.at[(CH - 1, 0)[d]]
            dest = con.at[(0, CH + 1)[d], own, :]
        else:
            source = con_in.at[:, pl.ds((CY - W4, 0)[d - 2], W4), :]
            dest = con.at[pl.ds(1, CH), pl.ds((O - W4, O + CY)[d - 2], W4), :]
        return pltpu.make_async_remote_copy(
            source, dest, ks.at[d], kr.at[d], device_id=peer[d], device_id_type=MESH
        )

    wide_rows = pl.ds(O - W4, CY + 2 * W4)
    wide_copy = pltpu.make_async_remote_copy(
        con.at[pl.ds(1, 4), wide_rows, :],
        kc.at[pl.ds(5, 4), wide_rows, :],
        ks.at[4],
        kr.at[4],
        device_id=lo_b,
        device_id_type=MESH,
    )
    r0_copy = pltpu.make_async_remote_copy(
        r0.at[pl.ds(0, 3)], r0_up, ks.at[5], kr.at[5], device_id=lo_b, device_id_type=MESH
    )
    dl_copy = pltpu.make_async_remote_copy(
        dup, dlow, ks.at[6], kr.at[6], device_id=hi_b, device_id_type=MESH
    )

    def edge_copy(d):
        source = hc.at[4, pl.ds((O + CY - W4, O)[d - 2], W4), :]
        dest = hc.at[4, pl.ds((O - W4, O + CY)[d - 2], W4), :]
        return pltpu.make_async_remote_copy(
            source, dest, ks.at[5 + d], kr.at[5 + d], device_id=peer[d], device_id_type=MESH
        )

    def go(cond, copy):
        @pl.when(cond)
        def _():
            copy.start()

    def arrived(cond, copy):
        @pl.when(cond)
        def _():
            copy.wait_recv()

    def left(cond, copy):
        @pl.when(cond)
        def _():
            copy.wait_send()

    def spread(send, recv, sem, block, rows):
        for k in range(nb - 1):
            step = (k + 1) // 2
            to = mb + (nb // 2 + (step if k % 2 == 1 else -step))
            to = jnp.where(to >= nb, to - nb, to)
            pltpu.make_async_remote_copy(
                send.at[pl.ds(to * block, rows), :] if block else send,
                recv.at[pl.ds(mb * max(block, rows), rows), :],
                as_.at[sem],
                ar.at[sem],
                device_id={"blk": to},
                device_id_type=MESH,
            ).start()

    def spread_waiter(send, recv, sem, rows):
        rows = pl.ds(0, (nb - 1) * rows)
        return pltpu.make_async_remote_copy(
            recv.at[rows, :], recv.at[rows, :], as_.at[sem], ar.at[sem], device_id=hi_b, device_id_type=MESH
        )

    for g in range(len(GROUPS)):
        for d in range(2):
            go(has[d], x_copy(0, d, g))
        for d in (2, 3):
            for x in (CX, 1):
                go(has[d], outer_copy(0, d, g, x))
    for g in range(len(GROUPS)):
        for d in (2, 3):
            go(has[d], inner_copy(0, d, g))
    for d in range(4):
        go(has[d], con_copy(d))
    for d in range(4):
        go(has[d], solid_copy(0, d, True))

    own_block = pl.ds(mb * slot, slot)
    loads[9].wait()
    loads[10].wait()
    ow = owner_v[...].astype(F32)
    tg = target_v[...].astype(F32)
    rows2 = lax.broadcasted_iota(jnp.int32, (CY, CY), 0)
    cols2 = lax.broadcasted_iota(jnp.int32, (CY, CY), 1)
    ow_l = jnp.broadcast_to(ow, (CY, CY))
    ow_s = jnp.sum(jnp.where(rows2 == cols2, ow_l, 0.0), axis=1, keepdims=True)
    same = jnp.where(jnp.broadcast_to(ow_s, (CY, CY)) == ow_l, 1.0, 0.0)
    rank_l = jnp.sum(jnp.where(rows2 < cols2, same, 0.0), axis=0, keepdims=True)
    rank_s = jnp.sum(jnp.where(cols2 < rows2, same, 0.0), axis=1, keepdims=True)
    slot_l = ow * float(slot) + rank_l
    slot_s = ow_s * float(slot) + rank_s
    p_rows = lax.broadcasted_iota(jnp.int32, (ns, CY), 0).astype(F32)
    hot = jnp.broadcast_to(slot_l, (ns, CY)) == p_rows
    pmat[...] = jnp.where(hot, 1.0, 0.0).astype(jnp.bfloat16)
    p_cols = lax.broadcasted_iota(jnp.int32, (CY, ns), 1).astype(F32)
    pmat_t[...] = jnp.where(jnp.broadcast_to(slot_s, (CY, ns)) == p_cols, 1.0, 0.0).astype(jnp.bfloat16)
    meta = jnp.sum(jnp.where(hot, jnp.broadcast_to(tg + 1.0, (ns, CY)), 0.0), axis=1, keepdims=True) - 1.0
    at_row = lax.broadcasted_iota(jnp.int32, (ns, NZ), 0)
    at_lane = lax.broadcasted_iota(jnp.int32, (ns, NZ), 1)
    slot_lane = lax.rem(at_row, slot) == at_lane
    block_of = lax.broadcasted_iota(jnp.int32, (nb, ns), 1) // slot == lax.broadcasted_iota(jnp.int32, (nb, ns), 0)
    spread_out = jnp.where(slot_lane, jnp.broadcast_to(meta, (ns, NZ)), 0.0).astype(jnp.bfloat16)
    msend[...] = jnp.dot(
        jnp.where(block_of, 1.0, 0.0).astype(jnp.bfloat16), spread_out, preferred_element_type=F32
    )
    own_row = pl.ds(mb, 1)
    mrecv[own_row, :] = msend[own_row, :]

    lane = lax.broadcasted_iota(jnp.int32, (CY, NZ), 1)
    first_lane, last_lane = lane == 0, lane == NZ - 1

    loads[1].wait()
    loads[7].wait()
    loads[8].wait()

    @pl.loop(0, CX)
    def _(x):
        total = vel[0, x] + vel[1, x] + vel[2, x]
        for f in range(NF):
            inv[f, x] = OMEGA / (total + (6.0 * dif[f] + jac[f, f]))

    for k in range(3):
        dl[k] = jnp.zeros((9, ROWS, NZ), F32)
    for p in range(9):
        if p != 4:
            hc[p] = jnp.zeros((ROWS, NZ), F32)
        kc[p, 0 : O - W4, :] = jnp.zeros((O - W4, NZ), F32)
        kc[p, O + CY + W4 : ROWS, :] = jnp.zeros((ROWS - O - CY - W4, NZ), F32)
    hc[4, 0 : O - W4, :] = jnp.zeros((O - W4, NZ), F32)
    hc[4, O + CY + W4 : ROWS, :] = jnp.zeros((ROWS - O - CY - W4, NZ), F32)

    def fluid_plane(e, x, fields=range(NF)):
        centre = [adj[e, f, x, O : O + CY, :] for f in range(NF)]
        u = [vel[i, x - 1] for i in range(3)]
        residuals = []
        for f in fields:
            c = centre[f]
            x_next = adj[e, f, x + 1, O : O + CY, :]
            y_next = adj[e, f, x, O + 1 : O + 1 + CY, :]
            z_next = jnp.where(last_lane, 0.0, pltpu.roll(c, NZ - 1, 1))
            z_back = jnp.where(first_lane, 0.0, pltpu.roll(c, 1, 1))
            near = (x_next + adj[e, f, x - 1, O : O + CY, :]) + (y_next + adj[e, f, x, O - 1 : O - 1 + CY, :])
            near = near + (z_next + z_back)
            flow = (dif[f] * near + u[0] * x_next) + (u[1] * y_next + u[2] * z_next)
            others = [g for g in range(NF) if g != f]
            mixing = (jac[f, others[0]] * centre[others[0]] + jac[f, others[1]] * centre[others[1]]) + (
                jac[f, others[2]] * centre[others[2]] + jac[f, others[3]] * centre[others[3]]
            )
            flow = (src[f, x - 1] + flow) - mixing
            if e == SWEEPS - 1:
                residual = flow - ((6.0 * dif[f] + jac[f, f]) + (u[0] + u[1] + u[2])) * c
                new = c + inv[f, x - 1] * residual
                residuals.append(residual)
            else:
                new = (1.0 - OMEGA) * c + inv[f, x - 1] * flow
            adj[e + 1, f, x, O : O + CY, :] = new
        return residuals

    def select(matrix, values):
        total = None
        for _ in range(3):
            part = values.astype(jnp.bfloat16)
            values = values - part.astype(F32)
            term = jnp.dot(matrix, part, preferred_element_type=F32)
            total = term if total is None else total + term
        return total

    def folded(values):
        return (values * values).reshape(CY // 8, 8, NZ).sum(axis=0)

    def flows2(q, k, gz, i, a, n):
        c, kk = q[i, pl.ds(a, n), :], k[i, pl.ds(a, n), :]
        flow = (kk + k[i + 1, pl.ds(a, n), :]) * q[i + 1, pl.ds(a, n), :]
        flow = flow + (kk + k[i - 1, pl.ds(a, n), :]) * q[i - 1, pl.ds(a, n), :]
        flow = flow + (kk + k[i, pl.ds(a + 1, n), :]) * q[i, pl.ds(a + 1, n), :]
        flow = flow + (kk + k[i, pl.ds(a - 1, n), :]) * q[i, pl.ds(a - 1, n), :]
        flow = flow + gz * pltpu.roll(c, NZ - 1, 1) + pltpu.roll(gz * c, 1, 1)
        return c, flow

    def coefficients(k, i, a, n):
        kk = k[i, pl.ds(a, n), :]
        at = lax.broadcasted_iota(jnp.int32, (n, NZ), 1)
        k_next = jnp.where(at == NZ - 1, 0.0, pltpu.roll(kk, NZ - 1, 1))
        k_back = jnp.where(at == 0, 0.0, pltpu.roll(kk, 1, 1))
        diagonal = 6.0 * kk + k[i + 1, pl.ds(a, n), :] + k[i - 1, pl.ds(a, n), :]
        diagonal = diagonal + k[i, pl.ds(a + 1, n), :] + k[i, pl.ds(a - 1, n), :] + k_next + k_back
        gz = jnp.where(at == NZ - 1, 0.0, kk + k_next)
        return gz, diagonal

    def solid_plane(e, p):
        c, flow = flows2(tem.at[e], con, sgz[p - 1], p, O, CY)
        if e < SWEEPS - 1:
            return None, (1.0 - OMEGA) * c + sdi[p - 1] * (heat[p - 1] + 0.5 * flow)
        residual = heat[p - 1] - 0.5 * (sd2[p - 1] * c - flow)
        return residual, c + sdi[p - 1] * residual

    def solid_prepare():
        loads[3].wait()
        for d in range(4):
            arrived(came[d], con_copy(d))

        @pl.loop(1, CH + 1)
        def _(p):
            gz, diagonal = coefficients(con, p, O, CY)
            sgz[p - 1] = gz
            sd2[p - 1] = diagonal
            sdi[p - 1] = (2.0 * OMEGA) / diagonal

    def solid_wait(e):
        for d in range(4):
            arrived(came[d], solid_copy(e, d, e == 0))

    def solid_sweep(e):
        def put(p):
            tem[e + 1, p, O : O + CY, :] = solid_plane(e, p)[1]

        put(1)
        put(CH)
        for d in range(2):
            go(has[d], solid_copy(e + 1, d))

        @pl.loop(2, CH)
        def _(p):
            put(p)

        for d in range(2, 4):
            go(has[d], solid_copy(e + 1, d))

    def outer_wait(e, g):
        for d in range(2):
            arrived(came[d], x_copy(e, d, g))
        for d in (2, 3):
            arrived(came[d], outer_copy(e, d, g, 1, 2))

    def inner_wait(e, g):
        for d in (2, 3):
            arrived(came[d], inner_copy(e, d, g))

    loads[0].wait()
    loads[2].wait()
    for e in range(SWEEPS - 1):
        for g in range(len(GROUPS)):
            outer_wait(e, g)
            for d, x in ((0, CX), (1, 1)):
                fluid_plane(e, x, range(GROUPS[g][0], sum(GROUPS[g])))
                go(has[d], x_copy(e + 1, d, g))
                for k in (2, 3):
                    go(has[k], outer_copy(e + 1, k, g, x))
            inner_wait(e, g)

            @pl.loop(2 + share * g, 2 + share * (g + 1))
            def _(x):
                fluid_plane(e, x)

            for k in (2, 3):
                go(has[k], inner_copy(e + 1, k, g))
            if e == 0 and g == 0:
                heard(0)
                greet(1)
            if e == 1 and g == 0:
                heard(2)
                greet(3)
        if e == 0:
            solid_prepare()
            loads[4].wait()
            loads[5].wait()
        solid_wait(e)
        solid_sweep(e)
        if e == 0:
            heard(1)
            greet(2)
        if e == 1:
            heard(3)
            spread(msend, mrecv, 0, 1, 1)
        if e == SWEEPS - 2:
            go(has_lo_b, wide_copy)

    n40 = CY + 2 * W4
    for p in range(5):
        kc[p, O - W4 : O + CY + W4, :] = con[12 + p, O - W4 : O + CY + W4, :]

    loads[6].wait()

    e = SWEEPS - 1
    arrived(came[0], x_copy(e, 0, 0))
    for d in (2, 3):
        arrived(came[d], outer_copy(e, d, 0, 1, 2))
    fluid_plane(e, 1, (NF - 1,))
    flux = wall[...] * adj[SWEEPS, NF - 1, 1, O : O + CY, :]
    fsend[...] = select(pmat[...], flux)
    spread(fsend, frecv, 1, slot, slot - 1)
    frecv[own_block, :] = fsend[own_block, :]

    arrived(came[1], x_copy(e, 1, 0))
    for g in range(1, len(GROUPS)):
        outer_wait(e, g)
    for g in range(len(GROUPS)):
        inner_wait(e, g)

    def more(x, carry):
        return tuple(a + folded(r) for a, r in zip(carry, fluid_plane(e, x)))

    zero8 = jnp.zeros((8, NZ), F32)
    squares = lax.fori_loop(1, CX + 1, more, (zero8,) * NF)
    outs = [
        pltpu.make_async_copy(
            adj.at[SWEEPS, pl.ds(0, NF - 1), pl.ds(1, CX), own, :], adj_out.at[pl.ds(0, NF - 1)], osem.at[0]
        ),
        pltpu.make_async_copy(
            adj.at[SWEEPS, NF - 1, pl.ds(2, CX - 1), own, :], adj_out.at[NF - 1, pl.ds(1, CX - 1)], osem.at[1]
        ),
    ]
    for copy in outs:
        copy.start()

    solid_wait(e)

    def edge(first, count, at):
        def body(i, carry):
            residual, new = solid_plane(e, first + i)
            tout[first + i - 1] = new
            r0[at + i] = residual
            return carry + folded(residual)

        return lax.fori_loop(0, count, body, zero8)

    low_squares = edge(1, 3, 0)
    go(has_lo_b, r0_copy)
    edge(13, 4, 3)

    def middle(p, carry):
        residual, new = solid_plane(e, p)
        tout[p - 1] = new
        return carry + folded(residual)

    solid_squares = lax.fori_loop(4, 13, middle, zero8)
    outs.append(pltpu.make_async_copy(tout.at[pl.ds(3, 9)], sol_out.at[pl.ds(3, 9)], osem.at[2]))
    outs[-1].start()
    solid_squares = solid_squares + jnp.where(has_lo_b, 0.0, low_squares)

    arrived(has_hi_b, wide_copy)
    row = lax.broadcasted_iota(jnp.int32, (n40, NZ), 0) - W4
    inside = (row >= jnp.where(has_lo_s, -3, 0)) & (row <= jnp.where(has_hi_s, CY + 2, CY - 1))

    @pl.loop(1, 8)
    def _(i):
        gz, diagonal = coefficients(kc, i, O - W4, n40)
        ok = inside & ((i < 5) | has_hi_b)
        cgz[i] = gz
        cd2[i] = diagonal
        cdi[i] = jnp.where(ok, (2.0 * OMEGA) / jnp.where(ok, diagonal, 1.0), 0.0)

    lane8 = lax.broadcasted_iota(jnp.int32, (8, NZ), 1)
    row8 = lax.broadcasted_iota(jnp.int32, (8, NZ), 0)
    sums = jnp.zeros((8, NZ), F32)
    for f in range(NF):
        sums = sums + jnp.where(row8 == f, jnp.broadcast_to(jnp.sum(squares[f], axis=0, keepdims=True), (8, NZ)), 0.0)

    spread_waiter(msend, mrecv, 0, 1).wait_recv()
    to_slot = lax.broadcasted_iota(jnp.int32, (ns, nb), 0) // slot == lax.broadcasted_iota(jnp.int32, (ns, nb), 1)
    rows_of = jnp.dot(
        jnp.where(to_slot, 1.0, 0.0).astype(jnp.bfloat16), mrecv[...].astype(jnp.bfloat16), preferred_element_type=F32
    )
    rows_of = jnp.sum(jnp.where(slot_lane, rows_of, 0.0), axis=1, keepdims=True)
    hit = jnp.where(jnp.broadcast_to(rows_of, (ns, NZ)) == at_lane.astype(F32), 1.0, 0.0)
    smat_t[...] = hit.astype(jnp.bfloat16)
    smat[...] = jnp.transpose(hit).astype(jnp.bfloat16)

    spread_waiter(fsend, frecv, 1, slot - 1).wait_recv()
    hc[4, O : O + CY, :] = select(smat[0:CY, :], frecv[...])
    for d in (2, 3):
        go(has[d], edge_copy(d))
    for d in (2, 3):
        arrived(came[d], edge_copy(d))
    arrived(has_hi_b, r0_copy)

    wide = slice(O - W4, O + CY + W4)
    dl[0, 4, wide, :] = cdi[4] * hc[4, wide, :]
    for k in range(2):

        @pl.loop(3 - k, 6 + k)
        def _(i):
            c, flow = flows2(dl.at[k], kc, cgz[i], i, O - W4, n40)
            dl[k + 1, i, wide, :] = c + cdi[i] * (hc[i, wide, :] - 0.5 * (cd2[i] * c - flow))

    mid = pl.ds(W4, CY)

    def last(i):
        c, flow = flows2(dl.at[2], kc, cgz[i, mid, :], i, O, CY)
        residual = hc[i, O : O + CY, :] - 0.5 * (cd2[i, mid, :] * c - flow)
        return residual, c + cdi[i, mid, :] * residual

    def last_own(i, carry):
        residual, delta = last(i)
        tout[11 + i] = tout[11 + i] + delta
        return carry + folded(residual + r0[2 + i])

    solid_squares = lax.fori_loop(1, 5, last_own, solid_squares)

    def last_up(i, carry):
        residual, delta = last(i)
        dup[i - 5] = delta
        return carry + folded(residual + r0_up[i - 5])

    up_squares = lax.fori_loop(5, 8, last_up, zero8)
    go(has_hi_b, dl_copy)
    solid_squares = solid_squares + jnp.where(has_hi_b, up_squares, 0.0)
    sums = sums + jnp.where(row8 == NF, jnp.broadcast_to(jnp.sum(solid_squares, axis=0, keepdims=True), (8, NZ)), 0.0)
    totals = jnp.broadcast_to(jnp.sum(sums, axis=1, keepdims=True), (8, NZ))
    totals = jnp.sum(jnp.where(row8 == lane8, totals, 0.0), axis=0, keepdims=True)

    nmine[...] = totals
    spread(nmine, nrow, 4, 0, 1)
    nrow[own_row, :] = totals
    rsend[...] = select(smat_t[:, 0:CY], tout[CH - 1])
    spread(rsend, rrecv, 2, slot, slot - 1)
    rrecv[own_block, :] = rsend[own_block, :]
    outs.append(pltpu.make_async_copy(tout.at[pl.ds(12, 4)], sol_out.at[pl.ds(12, 4)], osem.at[3]))
    outs[-1].start()

    arrived(has_lo_b, dl_copy)
    for i in range(3):
        tout[i] = tout[i] + dlow[i]
    outs.append(pltpu.make_async_copy(tout.at[pl.ds(0, 3)], sol_out.at[pl.ds(0, 3)], osem.at[4]))
    outs[-1].start()

    spread_waiter(nmine, nrow, 4, 1).wait_recv()
    nsend[...] = jnp.sum(nrow[...], axis=0, keepdims=True)

    def norm_copy(to):
        return pltpu.make_async_remote_copy(
            nsend, nrecv.at[ms], as_.at[3], ar.at[3], device_id={"span": to}, device_id_type=MESH
        )

    @pl.loop(1, nsp)
    def _(k):
        norm_copy(lax.rem(ms + k, nsp)).start()

    nrecv[ms] = nsend[...]
    spread_waiter(rsend, rrecv, 2, slot - 1).wait_recv()
    returned = select(pmat_t[...], rrecv[...])
    fin[...] = adj[SWEEPS, NF - 1, 1, O : O + CY, :] + wall[...] * returned
    outs.append(pltpu.make_async_copy(fin, adj_out.at[NF - 1, 0], osem.at[5]))
    outs[-1].start()

    norm_waiter = pltpu.make_async_remote_copy(
        nrecv.at[pl.ds(0, nsp - 1)],
        nrecv.at[pl.ds(0, nsp - 1)],
        as_.at[3],
        ar.at[3],
        device_id=hi_s,
        device_id_type=MESH,
    )
    norm_waiter.wait_recv()
    total = nrecv[0]
    for k in range(1, nsp):
        total = total + nrecv[k]
    cells = jnp.where(lane8 < NF, fluid_cells, solid_cells)
    norm_out[...] = jnp.sqrt(jnp.broadcast_to(total, (8, NZ)) / cells)

    for e in range(SWEEPS):
        for d in range(4):
            left(has[d], solid_copy(e, d, e == 0))
    for d in range(4):
        left(has[d], fluid_sent(d))
    for d in range(4):
        left(has[d], con_copy(d))
    left(has_lo_b, wide_copy)
    left(has_lo_b, r0_copy)
    left(has_hi_b, dl_copy)
    for d in (2, 3):
        left(has[d], edge_copy(d))
    spread_waiter(msend, mrecv, 0, 1).wait_send()
    spread_waiter(fsend, frecv, 1, slot - 1).wait_send()
    spread_waiter(rsend, rrecv, 2, slot - 1).wait_send()
    spread_waiter(nmine, nrow, 4, 1).wait_send()
    norm_waiter.wait_send()
    for copy in outs:
        copy.wait()


def write_kernel(adjoint, solid, norms, adjoint_out, solid_out, norms_out, sem):
    copies = [
        pltpu.make_async_copy(adjoint, adjoint_out, sem.at[0]),
        pltpu.make_async_copy(solid, solid_out, sem.at[1]),
    ]
    for copy in copies:
        copy.start()
    norms_out[...] = norms[0, 0 : NF + 1]
    for copy in copies:
        copy.wait()


def shards(
    nb,
    nsp,
    slot,
    fluid_adjoint_in,
    fluid_source,
    velocity,
    diffusion,
    jacobian,
    wall_coefficient,
    metal_costate_prior,
    solid_source,
    conductivity,
    tile_owner,
    tile_target,
):
    ns = nb * slot
    every = nb * nsp

    def stay(x):
        return pltpu.with_memory_space_constraint(x, pltpu.HBM)

    anywhere = pl.BlockSpec(memory_space=pl.ANY)
    vmem = pl.BlockSpec(memory_space=pltpu.VMEM)
    V = pltpu.VMEM
    n40 = CY + 2 * W4
    dma = pltpu.SemaphoreType.DMA
    scratch = [
        pltpu.SMEM((NF,), F32),
        pltpu.SMEM((NF, NF), F32),
        V((1, CY), jnp.int32),
        V((1, CY), jnp.int32),
        V((SWEEPS + 1, NF, CX + 2, ROWS, NZ), F32),
        V((NF, CX, CY, NZ), F32),
        V((3, CX, CY, NZ), F32),
        V((NF, CX, CY, NZ), F32),
        V((CY, NZ), F32),
        V((CY, NZ), F32),
        V((SWEEPS, CH + 2, ROWS, NZ), F32),
        V((CH + 2, ROWS, NZ), F32),
        V((CH, CY, NZ), F32),
        V((CH, CY, NZ), F32),
        V((CH, CY, NZ), F32),
        V((CH, CY, NZ), F32),
        V((CH, CY, NZ), F32),
        V((7, CY, NZ), F32),
        V((3, CY, NZ), F32),
        V((9, ROWS, NZ), F32),
        V((8, n40, NZ), F32),
        V((8, n40, NZ), F32),
        V((8, n40, NZ), F32),
        V((9, ROWS, NZ), F32),
        V((3, 9, ROWS, NZ), F32),
        V((3, CY, NZ), F32),
        V((3, CY, NZ), F32),
        V((ns, CY), jnp.bfloat16),
        V((CY, ns), jnp.bfloat16),
        V((NZ, ns), jnp.bfloat16),
        V((ns, NZ), jnp.bfloat16),
    ]
    scratch += [V((nb, NZ), F32)] * 2
    scratch += [V((ns, NZ), F32)] * 4
    scratch += [V((1, NZ), F32), V((nb, NZ), F32)]
    scratch += [V((1, NZ), F32), V((nsp, 1, NZ), F32)]
    scratch += [
        dma((11,)),
        dma((6,)),
        dma((2,)),
        dma((SWEEPS, 2, len(GROUPS))),
        dma((2,)),
        dma((SWEEPS, 2, len(GROUPS))),
        dma((SWEEPS, 2, len(GROUPS))),
        dma((SWEEPS, 4)),
        dma((SWEEPS, 4)),
        dma((9,)),
        dma((9,)),
        dma((1,)),
        dma((1,)),
        dma((5,)),
        dma((5,)),
        pltpu.SemaphoreType.REGULAR((8,)),
        pltpu.SemaphoreType.REGULAR((8,)),
    ]
    adjoint, solid, norms = pl.pallas_call(
        functools.partial(
            kernel, nb, nsp, slot, float(CX * CY * NZ * every), float(CH * CY * NZ * every)
        ),
        out_shape=(
            jax.ShapeDtypeStruct(fluid_adjoint_in.shape, F32),
            jax.ShapeDtypeStruct(metal_costate_prior.shape, F32),
            jax.ShapeDtypeStruct((8, NZ), F32),
        ),
        in_specs=[anywhere] * 11,
        out_specs=(anywhere, anywhere, vmem),
        scratch_shapes=scratch,
        compiler_params=pltpu.CompilerParams(collective_id=0, has_side_effects=True, vmem_limit_bytes=24 * 2**20),
        name="iteration",
    )(
        *map(
            stay,
            (
                fluid_adjoint_in,
                fluid_source,
                velocity,
                diffusion,
                jacobian,
                wall_coefficient,
                metal_costate_prior,
                solid_source,
                conductivity,
                tile_owner.reshape(1, CY),
                tile_target,
            ),
        )
    )
    hbm = pl.BlockSpec(memory_space=pltpu.HBM)
    return pl.pallas_call(
        write_kernel,
        out_shape=(
            jax.ShapeDtypeStruct(fluid_adjoint_in.shape, F32),
            jax.ShapeDtypeStruct(metal_costate_prior.shape, F32),
            jax.ShapeDtypeStruct((NF + 1,), F32),
        ),
        in_specs=[vmem, vmem, vmem],
        out_specs=(hbm, hbm, vmem),
        scratch_shapes=[dma((2,))],
        compiler_params=pltpu.CompilerParams(vmem_limit_bytes=24 * 2**20),
        name="write",
    )(adjoint, solid, norms)


def solution(mesh, slot=4):
    placed = (
        P(None, "blk", "span", None),
        P(None, "blk", "span", None),
        P(None, "blk", "span", None),
        P(),
        P(),
        P("blk", "span", None),
        P("blk", "span", None),
        P("blk", "span", None),
        P("blk", "span", None),
        P("span", "blk", None),
        P("span", "blk"),
    )
    return jax.shard_map(
        functools.partial(shards, mesh.shape["blk"], mesh.shape["span"], slot),
        mesh=mesh,
        in_specs=placed,
        out_specs=(P(None, "blk", "span", None), P("blk", "span", None), P()),
        check_vma=False,
    )
```

```python
import functools

import jax
import jax.numpy as jnp
from jax import lax
from jax.experimental import pallas as pl
from jax.experimental.pallas import tpu as pltpu
from jax.sharding import PartitionSpec as P

MESH = pl.DeviceIdType.MESH
F32 = jnp.float32
NF = 5
CX = 8
CY = 32
CH = 16
NZ = 128
ROWS = 48
O = 8
W4 = 4
SWEEPS = 4
OMEGA = 0.8
GROUPS = ((4, 1), (2, 2), (0, 2))


def kernel(
    nb,
    nsp,
    slot,
    fluid_cells,
    solid_cells,
    adj_in,
    src_in,
    vel_in,
    dif_in,
    jac_in,
    wall_in,
    tem_in,
    heat_in,
    con_in,
    owner_in,
    target_in,
    adj_out,
    sol_out,
    norm_out,
    dif,
    jac,
    owner_v,
    target_v,
    adj,
    src,
    vel,
    inv,
    wall,
    fin,
    tem,
    con,
    heat,
    sgz,
    sd2,
    sdi,
    tout,
    r0,
    r0_up,
    kc,
    cgz,
    cd2,
    cdi,
    hc,
    dl,
    dup,
    dlow,
    pmat,
    pmat_t,
    smat,
    smat_t,
    msend,
    mrecv,
    fsend,
    frecv,
    rsend,
    rrecv,
    nmine,
    nrow,
    nsend,
    nrecv,
    lsem,
    osem,
    xfs,
    xfr,
    yfs,
    ybr,
    yir,
    ts,
    tr,
    ks,
    kr,
    xs,
    xr,
    as_,
    ar,
    gb,
    gs,
):
    ns = nb * slot
    mb = lax.axis_index("blk")
    ms = lax.axis_index("span")
    has_lo_b, has_hi_b = mb > 0, mb < nb - 1
    has_lo_s, has_hi_s = ms > 0, ms < nsp - 1
    lo_b, hi_b = {"blk": mb - 1}, {"blk": mb + 1}
    lo_s, hi_s = {"span": ms - 1}, {"span": ms + 1}
    has = (has_hi_b, has_lo_b, has_hi_s, has_lo_s)
    came = (has_lo_b, has_hi_b, has_lo_s, has_hi_s)
    peer = (hi_b, lo_b, hi_s, lo_s)

    own = pl.ds(O, CY)

    frecv[...] = jnp.zeros_like(frecv)
    rrecv[...] = jnp.zeros_like(rrecv)

    barrier = pltpu.get_barrier_semaphore()

    def around(axis, me, n, distance, sem):
        for to in (lax.rem(me + distance, n), lax.rem(me + n - distance, n)):
            pl.semaphore_signal(sem, inc=1, device_id={axis: to}, device_id_type=MESH)

    around("blk", mb, nb, 1, barrier)
    around("span", ms, nsp, 1, barrier)

    def rounds(n):
        return max(0, (n // 2 - 1).bit_length())

    def greet(j):
        if j < rounds(nb):
            around("blk", mb, nb, 2**j, gb.at[j])
        if j < rounds(nsp):
            around("span", ms, nsp, 2**j, gs.at[j])

    def heard(j):
        if j < rounds(nb):
            pl.semaphore_wait(gb.at[j], 2)
        if j < rounds(nsp):
            pl.semaphore_wait(gs.at[j], 2)

    loads = [
        pltpu.make_async_copy(adj_in, adj.at[0, :, pl.ds(1, CX), own, :], lsem.at[0]),
        pltpu.make_async_copy(vel_in, vel, lsem.at[1]),
        pltpu.make_async_copy(src_in, src, lsem.at[2]),
        pltpu.make_async_copy(con_in, con.at[pl.ds(1, CH), own, :], lsem.at[3]),
        pltpu.make_async_copy(tem_in, tem.at[0, pl.ds(1, CH), own, :], lsem.at[4]),
        pltpu.make_async_copy(heat_in, heat, lsem.at[5]),
        pltpu.make_async_copy(wall_in.at[0], wall, lsem.at[6]),
        pltpu.make_async_copy(dif_in, dif, lsem.at[7]),
        pltpu.make_async_copy(jac_in, jac, lsem.at[8]),
        pltpu.make_async_copy(owner_in, owner_v, lsem.at[9]),
        pltpu.make_async_copy(target_in, target_v, lsem.at[10]),
    ]
    for copy in loads:
        copy.start()

    def zero_halos(cond, put):
        @pl.when(jnp.logical_not(cond))
        def _():
            put()

    def z_lo_b():
        for e in range(SWEEPS):
            adj[e, :, 0, O : O + CY, :] = jnp.zeros((NF, CY, NZ), F32)
            tem[e, 0, O : O + CY, :] = jnp.zeros((CY, NZ), F32)
        con[0, O : O + CY, :] = jnp.zeros((CY, NZ), F32)
        dlow[...] = jnp.zeros_like(dlow)

    def z_hi_b():
        for e in range(SWEEPS):
            adj[e, :, CX + 1, O : O + CY, :] = jnp.zeros((NF, CY, NZ), F32)
            tem[e, CH + 1, O : O + CY, :] = jnp.zeros((CY, NZ), F32)
        con[CH + 1, O : O + CY, :] = jnp.zeros((CY, NZ), F32)
        kc[5:9, O - W4 : O + CY + W4, :] = jnp.zeros((4, CY + 2 * W4, NZ), F32)
        r0_up[...] = jnp.zeros_like(r0_up)

    def z_span(halo, wide):
        def put():
            for e in range(SWEEPS):
                adj[e, :, 1 : CX + 1, halo : halo + 1, :] = jnp.zeros((NF, CX, 1, NZ), F32)
                tem[e, 1 : CH + 1, halo : halo + 1, :] = jnp.zeros((CH, 1, NZ), F32)
            con[1 : CH + 1, wide : wide + W4, :] = jnp.zeros((CH, W4, NZ), F32)
            hc[4, wide : wide + W4, :] = jnp.zeros((W4, NZ), F32)

        return put

    zero_halos(has_lo_b, z_lo_b)
    zero_halos(has_hi_b, z_hi_b)
    zero_halos(has_lo_s, z_span(O - 1, O - W4))
    zero_halos(has_hi_s, z_span(O + CY, O + CY))

    pl.semaphore_wait(barrier, 4)
    greet(0)

    share = (CX - 2) // len(GROUPS)

    def x_copy(e, d, g):
        plane, fields = (CX, 1)[d], pl.ds(*GROUPS[g])
        return pltpu.make_async_remote_copy(
            adj_in.at[fields, plane - 1] if e == 0 else adj.at[e, fields, plane, own, :],
            adj.at[e, fields, (0, CX + 1)[d], own, :],
            xfs.at[d],
            xfr.at[e, d, g],
            device_id=peer[d],
            device_id_type=MESH,
        )

    def y_copy(e, d, fields, planes, sem):
        row, halo = (CY - 1, 0)[d - 2], (O - 1, O + CY)[d - 2]
        inner = pl.ds(planes.start - 1, planes.size)
        return pltpu.make_async_remote_copy(
            adj_in.at[fields, inner, pl.ds(row, 1), :]
            if e == 0
            else adj.at[e, fields, planes, pl.ds(O + row, 1), :],
            adj.at[e, fields, planes, pl.ds(halo, 1), :],
            yfs.at[d - 2],
            sem,
            device_id=peer[d],
            device_id_type=MESH,
        )

    def outer_copy(e, d, g, x, count=1):
        return y_copy(e, d, pl.ds(*GROUPS[g]), pl.ds(x, count), ybr.at[e, d - 2, g])

    def inner_copy(e, d, g):
        return y_copy(e, d, pl.ds(0, NF), pl.ds(2 + share * g, share), yir.at[e, d - 2, g])

    def fluid_sent(d):
        ref = src.at[:, pl.ds(0, SWEEPS)] if d < 2 else src.at[:, 0]
        return pltpu.make_async_remote_copy(
            ref, ref, xfs.at[d] if d < 2 else yfs.at[d - 2], xfr.at[0, 0, 0], device_id=peer[d], device_id_type=MESH
        )

    def solid_copy(e, d, first=False):
        if d < 2:
            plane = (CH, 1)[d]
            source = tem_in.at[plane - 1] if first else tem.at[e, plane, own, :]
            dest = tem.at[e, (0, CH + 1)[d], own, :]
        else:
            row = (CY - 1, 0)[d - 2]
            source = (
                tem_in.at[:, pl.ds(row, 1), :]
                if first
                else tem.at[e, pl.ds(1, CH), pl.ds(O + row, 1), :]
            )
            dest = tem.at[e, pl.ds(1, CH), pl.ds((O - 1, O + CY)[d - 2], 1), :]
        return pltpu.make_async_remote_copy(
            source, dest, ts.at[e, d], tr.at[e, d], device_id=peer[d], device_id_type=MESH
        )

    def con_copy(d):
        if d < 2:
            source = con_in.at[(CH - 1, 0)[d]]
            dest = con.at[(0, CH + 1)[d], own, :]
        else:
            source = con_in.at[:, pl.ds((CY - W4, 0)[d - 2], W4), :]
            dest = con.at[pl.ds(1, CH), pl.ds((O - W4, O + CY)[d - 2], W4), :]
        return pltpu.make_async_remote_copy(
            source, dest, ks.at[d], kr.at[d], device_id=peer[d], device_id_type=MESH
        )

    wide_rows = pl.ds(O - W4, CY + 2 * W4)
    wide_copy = pltpu.make_async_remote_copy(
        con.at[pl.ds(1, 4), wide_rows, :],
        kc.at[pl.ds(5, 4), wide_rows, :],
        ks.at[4],
        kr.at[4],
        device_id=lo_b,
        device_id_type=MESH,
    )
    r0_copy = pltpu.make_async_remote_copy(
        r0.at[pl.ds(0, 3)], r0_up, ks.at[5], kr.at[5], device_id=lo_b, device_id_type=MESH
    )
    dl_copy = pltpu.make_async_remote_copy(
        dup, dlow, ks.at[6], kr.at[6], device_id=hi_b, device_id_type=MESH
    )

    def edge_copy(d):
        source = hc.at[4, pl.ds((O + CY - W4, O)[d - 2], W4), :]
        dest = hc.at[4, pl.ds((O - W4, O + CY)[d - 2], W4), :]
        return pltpu.make_async_remote_copy(
            source, dest, ks.at[5 + d], kr.at[5 + d], device_id=peer[d], device_id_type=MESH
        )

    def go(cond, copy):
        @pl.when(cond)
        def _():
            copy.start()

    def arrived(cond, copy):
        @pl.when(cond)
        def _():
            copy.wait_recv()

    def left(cond, copy):
        @pl.when(cond)
        def _():
            copy.wait_send()

    def spread(send, recv, sem, block, rows):
        for k in range(nb - 1):
            step = (k + 1) // 2
            to = mb + (nb // 2 + (step if k % 2 == 1 else -step))
            to = jnp.where(to >= nb, to - nb, to)
            pltpu.make_async_remote_copy(
                send.at[pl.ds(to * block, rows), :] if block else send,
                recv.at[pl.ds(mb * max(block, rows), rows), :],
                as_.at[sem],
                ar.at[sem],
                device_id={"blk": to},
                device_id_type=MESH,
            ).start()

    def spread_waiter(send, recv, sem, rows):
        rows = pl.ds(0, (nb - 1) * rows)
        return pltpu.make_async_remote_copy(
            recv.at[rows, :], recv.at[rows, :], as_.at[sem], ar.at[sem], device_id=hi_b, device_id_type=MESH
        )

    for g in range(len(GROUPS)):
        for d in range(2):
            go(has[d], x_copy(0, d, g))
        for d in (2, 3):
            for x in (CX, 1):
                go(has[d], outer_copy(0, d, g, x))
    for g in range(len(GROUPS)):
        for d in (2, 3):
            go(has[d], inner_copy(0, d, g))
    for d in range(4):
        go(has[d], con_copy(d))
    for d in range(4):
        go(has[d], solid_copy(0, d, True))

    own_block = pl.ds(mb * slot, slot)
    loads[9].wait()
    loads[10].wait()
    ow = owner_v[...].astype(F32)
    tg = target_v[...].astype(F32)
    rows2 = lax.broadcasted_iota(jnp.int32, (CY, CY), 0)
    cols2 = lax.broadcasted_iota(jnp.int32, (CY, CY), 1)
    ow_l = jnp.broadcast_to(ow, (CY, CY))
    ow_s = jnp.sum(jnp.where(rows2 == cols2, ow_l, 0.0), axis=1, keepdims=True)
    same = jnp.where(jnp.broadcast_to(ow_s, (CY, CY)) == ow_l, 1.0, 0.0)
    rank_l = jnp.sum(jnp.where(rows2 < cols2, same, 0.0), axis=0, keepdims=True)
    rank_s = jnp.sum(jnp.where(cols2 < rows2, same, 0.0), axis=1, keepdims=True)
    slot_l = ow * float(slot) + rank_l
    slot_s = ow_s * float(slot) + rank_s
    p_rows = lax.broadcasted_iota(jnp.int32, (ns, CY), 0).astype(F32)
    hot = jnp.broadcast_to(slot_l, (ns, CY)) == p_rows
    pmat[...] = jnp.where(hot, 1.0, 0.0).astype(jnp.bfloat16)
    p_cols = lax.broadcasted_iota(jnp.int32, (CY, ns), 1).astype(F32)
    pmat_t[...] = jnp.where(jnp.broadcast_to(slot_s, (CY, ns)) == p_cols, 1.0, 0.0).astype(jnp.bfloat16)
    meta = jnp.sum(jnp.where(hot, jnp.broadcast_to(tg + 1.0, (ns, CY)), 0.0), axis=1, keepdims=True) - 1.0
    at_row = lax.broadcasted_iota(jnp.int32, (ns, NZ), 0)
    at_lane = lax.broadcasted_iota(jnp.int32, (ns, NZ), 1)
    slot_lane = lax.rem(at_row, slot) == at_lane
    block_of = lax.broadcasted_iota(jnp.int32, (nb, ns), 1) // slot == lax.broadcasted_iota(jnp.int32, (nb, ns), 0)
    spread_out = jnp.where(slot_lane, jnp.broadcast_to(meta, (ns, NZ)), 0.0).astype(jnp.bfloat16)
    msend[...] = jnp.dot(
        jnp.where(block_of, 1.0, 0.0).astype(jnp.bfloat16), spread_out, preferred_element_type=F32
    )
    own_row = pl.ds(mb, 1)
    mrecv[own_row, :] = msend[own_row, :]

    lane = lax.broadcasted_iota(jnp.int32, (CY, NZ), 1)
    first_lane, last_lane = lane == 0, lane == NZ - 1

    loads[1].wait()
    loads[7].wait()
    loads[8].wait()

    @pl.loop(0, CX)
    def _(x):
        total = vel[0, x] + vel[1, x] + vel[2, x]
        for f in range(NF):
            inv[f, x] = OMEGA / (total + (6.0 * dif[f] + jac[f, f]))

    for k in range(3):
        dl[k] = jnp.zeros((9, ROWS, NZ), F32)
    for p in range(9):
        if p != 4:
            hc[p] = jnp.zeros((ROWS, NZ), F32)
        kc[p, 0 : O - W4, :] = jnp.zeros((O - W4, NZ), F32)
        kc[p, O + CY + W4 : ROWS, :] = jnp.zeros((ROWS - O - CY - W4, NZ), F32)
    hc[4, 0 : O - W4, :] = jnp.zeros((O - W4, NZ), F32)
    hc[4, O + CY + W4 : ROWS, :] = jnp.zeros((ROWS - O - CY - W4, NZ), F32)

    def fluid_plane(e, x, fields=range(NF)):
        centre = [adj[e, f, x, O : O + CY, :] for f in range(NF)]
        u = [vel[i, x - 1] for i in range(3)]
        residuals = []
        for f in fields:
            c = centre[f]
            x_next = adj[e, f, x + 1, O : O + CY, :]
            y_next = adj[e, f, x, O + 1 : O + 1 + CY, :]
            z_next = jnp.where(last_lane, 0.0, pltpu.roll(c, NZ - 1, 1))
            z_back = jnp.where(first_lane, 0.0, pltpu.roll(c, 1, 1))
            near = (x_next + adj[e, f, x - 1, O : O + CY, :]) + (y_next + adj[e, f, x, O - 1 : O - 1 + CY, :])
            near = near + (z_next + z_back)
            flow = (dif[f] * near + u[0] * x_next) + (u[1] * y_next + u[2] * z_next)
            others = [g for g in range(NF) if g != f]
            mixing = (jac[f, others[0]] * centre[others[0]] + jac[f, others[1]] * centre[others[1]]) + (
                jac[f, others[2]] * centre[others[2]] + jac[f, others[3]] * centre[others[3]]
            )
            flow = (src[f, x - 1] + flow) - mixing
            if e == SWEEPS - 1:
                residual = flow - ((6.0 * dif[f] + jac[f, f]) + (u[0] + u[1] + u[2])) * c
                new = c + inv[f, x - 1] * residual
                residuals.append(residual)
            else:
                new = (1.0 - OMEGA) * c + inv[f, x - 1] * flow
            adj[e + 1, f, x, O : O + CY, :] = new
        return residuals

    def select(matrix, values):
        total = None
        for _ in range(3):
            part = values.astype(jnp.bfloat16)
            values = values - part.astype(F32)
            term = jnp.dot(matrix, part, preferred_element_type=F32)
            total = term if total is None else total + term
        return total

    def folded(values):
        return (values * values).reshape(CY // 8, 8, NZ).sum(axis=0)

    def flows2(q, k, gz, i, a, n):
        c, kk = q[i, pl.ds(a, n), :], k[i, pl.ds(a, n), :]
        flow = (kk + k[i + 1, pl.ds(a, n), :]) * q[i + 1, pl.ds(a, n), :]
        flow = flow + (kk + k[i - 1, pl.ds(a, n), :]) * q[i - 1, pl.ds(a, n), :]
        flow = flow + (kk + k[i, pl.ds(a + 1, n), :]) * q[i, pl.ds(a + 1, n), :]
        flow = flow + (kk + k[i, pl.ds(a - 1, n), :]) * q[i, pl.ds(a - 1, n), :]
        flow = flow + gz * pltpu.roll(c, NZ - 1, 1) + pltpu.roll(gz * c, 1, 1)
        return c, flow

    def coefficients(k, i, a, n):
        kk = k[i, pl.ds(a, n), :]
        at = lax.broadcasted_iota(jnp.int32, (n, NZ), 1)
        k_next = jnp.where(at == NZ - 1, 0.0, pltpu.roll(kk, NZ - 1, 1))
        k_back = jnp.where(at == 0, 0.0, pltpu.roll(kk, 1, 1))
        diagonal = 6.0 * kk + k[i + 1, pl.ds(a, n), :] + k[i - 1, pl.ds(a, n), :]
        diagonal = diagonal + k[i, pl.ds(a + 1, n), :] + k[i, pl.ds(a - 1, n), :] + k_next + k_back
        gz = jnp.where(at == NZ - 1, 0.0, kk + k_next)
        return gz, diagonal

    def solid_plane(e, p):
        c, flow = flows2(tem.at[e], con, sgz[p - 1], p, O, CY)
        if e < SWEEPS - 1:
            return None, (1.0 - OMEGA) * c + sdi[p - 1] * (heat[p - 1] + 0.5 * flow)
        residual = heat[p - 1] - 0.5 * (sd2[p - 1] * c - flow)
        return residual, c + sdi[p - 1] * residual

    def solid_prepare():
        loads[3].wait()
        for d in range(4):
            arrived(came[d], con_copy(d))

        @pl.loop(1, CH + 1)
        def _(p):
            gz, diagonal = coefficients(con, p, O, CY)
            sgz[p - 1] = gz
            sd2[p - 1] = diagonal
            sdi[p - 1] = (2.0 * OMEGA) / diagonal

    def solid_wait(e):
        for d in range(4):
            arrived(came[d], solid_copy(e, d, e == 0))

    def solid_sweep(e):
        def put(p):
            tem[e + 1, p, O : O + CY, :] = solid_plane(e, p)[1]

        put(1)
        put(CH)
        for d in range(2):
            go(has[d], solid_copy(e + 1, d))

        @pl.loop(2, CH)
        def _(p):
            put(p)

        for d in range(2, 4):
            go(has[d], solid_copy(e + 1, d))

    def outer_wait(e, g):
        for d in range(2):
            arrived(came[d], x_copy(e, d, g))
        for d in (2, 3):
            arrived(came[d], outer_copy(e, d, g, 1, 2))

    def inner_wait(e, g):
        for d in (2, 3):
            arrived(came[d], inner_copy(e, d, g))

    loads[0].wait()
    loads[2].wait()
    for e in range(SWEEPS - 1):
        for g in range(len(GROUPS)):
            outer_wait(e, g)
            for d, x in ((0, CX), (1, 1)):
                fluid_plane(e, x, range(GROUPS[g][0], sum(GROUPS[g])))
                go(has[d], x_copy(e + 1, d, g))
                for k in (2, 3):
                    go(has[k], outer_copy(e + 1, k, g, x))
            inner_wait(e, g)

            @pl.loop(2 + share * g, 2 + share * (g + 1))
            def _(x):
                fluid_plane(e, x)

            for k in (2, 3):
                go(has[k], inner_copy(e + 1, k, g))
            if e == 0 and g == 0:
                heard(0)
                greet(1)
            if e == 1 and g == 0:
                heard(2)
                greet(3)
        if e == 0:
            solid_prepare()
            loads[4].wait()
            loads[5].wait()
        solid_wait(e)
        solid_sweep(e)
        if e == 0:
            heard(1)
            greet(2)
        if e == 1:
            heard(3)
            spread(msend, mrecv, 0, 1, 1)
        if e == SWEEPS - 2:
            go(has_lo_b, wide_copy)

    n40 = CY + 2 * W4
    for p in range(5):
        kc[p, O - W4 : O + CY + W4, :] = con[12 + p, O - W4 : O + CY + W4, :]

    loads[6].wait()

    e = SWEEPS - 1
    arrived(came[0], x_copy(e, 0, 0))
    for d in (2, 3):
        arrived(came[d], outer_copy(e, d, 0, 1, 2))
    fluid_plane(e, 1, (NF - 1,))
    flux = wall[...] * adj[SWEEPS, NF - 1, 1, O : O + CY, :]
    fsend[...] = select(pmat[...], flux)
    spread(fsend, frecv, 1, slot, slot - 1)
    frecv[own_block, :] = fsend[own_block, :]

    arrived(came[1], x_copy(e, 1, 0))
    for g in range(1, len(GROUPS)):
        outer_wait(e, g)
    for g in range(len(GROUPS)):
        inner_wait(e, g)

    def more(x, carry):
        return tuple(a + folded(r) for a, r in zip(carry, fluid_plane(e, x)))

    zero8 = jnp.zeros((8, NZ), F32)
    squares = lax.fori_loop(1, CX + 1, more, (zero8,) * NF)
    outs = [
        pltpu.make_async_copy(
            adj.at[SWEEPS, pl.ds(0, NF - 1), pl.ds(1, CX), own, :], adj_out.at[pl.ds(0, NF - 1)], osem.at[0]
        ),
        pltpu.make_async_copy(
            adj.at[SWEEPS, NF - 1, pl.ds(2, CX - 1), own, :], adj_out.at[NF - 1, pl.ds(1, CX - 1)], osem.at[1]
        ),
    ]
    for copy in outs:
        copy.start()

    solid_wait(e)

    def edge(first, count, at):
        def body(i, carry):
            residual, new = solid_plane(e, first + i)
            tout[first + i - 1] = new
            r0[at + i] = residual
            return carry + folded(residual)

        return lax.fori_loop(0, count, body, zero8)

    low_squares = edge(1, 3, 0)
    go(has_lo_b, r0_copy)
    edge(13, 4, 3)

    def middle(p, carry):
        residual, new = solid_plane(e, p)
        tout[p - 1] = new
        return carry + folded(residual)

    solid_squares = lax.fori_loop(4, 13, middle, zero8)
    outs.append(pltpu.make_async_copy(tout.at[pl.ds(3, 9)], sol_out.at[pl.ds(3, 9)], osem.at[2]))
    outs[-1].start()
    solid_squares = solid_squares + jnp.where(has_lo_b, 0.0, low_squares)

    arrived(has_hi_b, wide_copy)
    row = lax.broadcasted_iota(jnp.int32, (n40, NZ), 0) - W4
    inside = (row >= jnp.where(has_lo_s, -3, 0)) & (row <= jnp.where(has_hi_s, CY + 2, CY - 1))

    @pl.loop(1, 8)
    def _(i):
        gz, diagonal = coefficients(kc, i, O - W4, n40)
        ok = inside & ((i < 5) | has_hi_b)
        cgz[i] = gz
        cd2[i] = diagonal
        cdi[i] = jnp.where(ok, (2.0 * OMEGA) / jnp.where(ok, diagonal, 1.0), 0.0)

    lane8 = lax.broadcasted_iota(jnp.int32, (8, NZ), 1)
    row8 = lax.broadcasted_iota(jnp.int32, (8, NZ), 0)
    sums = jnp.zeros((8, NZ), F32)
    for f in range(NF):
        sums = sums + jnp.where(row8 == f, jnp.broadcast_to(jnp.sum(squares[f], axis=0, keepdims=True), (8, NZ)), 0.0)

    spread_waiter(msend, mrecv, 0, 1).wait_recv()
    to_slot = lax.broadcasted_iota(jnp.int32, (ns, nb), 0) // slot == lax.broadcasted_iota(jnp.int32, (ns, nb), 1)
    rows_of = jnp.dot(
        jnp.where(to_slot, 1.0, 0.0).astype(jnp.bfloat16), mrecv[...].astype(jnp.bfloat16), preferred_element_type=F32
    )
    rows_of = jnp.sum(jnp.where(slot_lane, rows_of, 0.0), axis=1, keepdims=True)
    hit = jnp.where(jnp.broadcast_to(rows_of, (ns, NZ)) == at_lane.astype(F32), 1.0, 0.0)
    smat_t[...] = hit.astype(jnp.bfloat16)
    smat[...] = jnp.transpose(hit).astype(jnp.bfloat16)

    spread_waiter(fsend, frecv, 1, slot - 1).wait_recv()
    hc[4, O : O + CY, :] = select(smat[0:CY, :], frecv[...])
    for d in (2, 3):
        go(has[d], edge_copy(d))
    for d in (2, 3):
        arrived(came[d], edge_copy(d))

    wide = slice(O - W4, O + CY + W4)
    dl[0, 4, wide, :] = cdi[4] * hc[4, wide, :]
    for k in range(2):

        @pl.loop(3 - k, 6 + k)
        def _(i):
            c, flow = flows2(dl.at[k], kc, cgz[i], i, O - W4, n40)
            dl[k + 1, i, wide, :] = c + cdi[i] * (hc[i, wide, :] - 0.5 * (cd2[i] * c - flow))

    mid = pl.ds(W4, CY)

    def last(i):
        c, flow = flows2(dl.at[2], kc, cgz[i, mid, :], i, O, CY)
        residual = hc[i, O : O + CY, :] - 0.5 * (cd2[i, mid, :] * c - flow)
        return residual, c + cdi[i, mid, :] * residual

    def last_own(i, carry):
        residual, delta = last(i)
        tout[11 + i] = tout[11 + i] + delta
        return carry + folded(residual + r0[2 + i])

    solid_squares = lax.fori_loop(1, 5, last_own, solid_squares)

    def last_up(i, carry):
        residual, delta = last(i)
        dup[i - 5] = delta
        return carry + folded(residual + r0_up[i - 5])

    arrived(has_hi_b, r0_copy)
    up_squares = lax.fori_loop(5, 8, last_up, zero8)
    go(has_hi_b, dl_copy)
    solid_squares = solid_squares + jnp.where(has_hi_b, up_squares, 0.0)
    sums = sums + jnp.where(row8 == NF, jnp.broadcast_to(jnp.sum(solid_squares, axis=0, keepdims=True), (8, NZ)), 0.0)
    totals = jnp.broadcast_to(jnp.sum(sums, axis=1, keepdims=True), (8, NZ))
    totals = jnp.sum(jnp.where(row8 == lane8, totals, 0.0), axis=0, keepdims=True)

    nmine[...] = totals
    spread(nmine, nrow, 4, 0, 1)
    nrow[own_row, :] = totals
    rsend[...] = select(smat_t[:, 0:CY], tout[CH - 1])
    spread(rsend, rrecv, 2, slot, slot - 1)
    rrecv[own_block, :] = rsend[own_block, :]
    outs.append(pltpu.make_async_copy(tout.at[pl.ds(12, 4)], sol_out.at[pl.ds(12, 4)], osem.at[3]))
    outs[-1].start()

    arrived(has_lo_b, dl_copy)
    for i in range(3):
        tout[i] = tout[i] + dlow[i]
    outs.append(pltpu.make_async_copy(tout.at[pl.ds(0, 3)], sol_out.at[pl.ds(0, 3)], osem.at[4]))
    outs[-1].start()

    spread_waiter(nmine, nrow, 4, 1).wait_recv()
    nsend[...] = jnp.sum(nrow[...], axis=0, keepdims=True)

    def norm_copy(to):
        return pltpu.make_async_remote_copy(
            nsend, nrecv.at[ms], as_.at[3], ar.at[3], device_id={"span": to}, device_id_type=MESH
        )

    @pl.loop(1, nsp)
    def _(k):
        norm_copy(lax.rem(ms + k, nsp)).start()

    nrecv[ms] = nsend[...]
    spread_waiter(rsend, rrecv, 2, slot - 1).wait_recv()
    returned = select(pmat_t[...], rrecv[...])
    fin[...] = adj[SWEEPS, NF - 1, 1, O : O + CY, :] + wall[...] * returned
    outs.append(pltpu.make_async_copy(fin, adj_out.at[NF - 1, 0], osem.at[5]))
    outs[-1].start()

    norm_waiter = pltpu.make_async_remote_copy(
        nrecv.at[pl.ds(0, nsp - 1)],
        nrecv.at[pl.ds(0, nsp - 1)],
        as_.at[3],
        ar.at[3],
        device_id=hi_s,
        device_id_type=MESH,
    )
    norm_waiter.wait_recv()
    total = nrecv[0]
    for k in range(1, nsp):
        total = total + nrecv[k]
    cells = jnp.where(lane8 < NF, fluid_cells, solid_cells)
    norm_out[...] = jnp.sqrt(jnp.broadcast_to(total, (8, NZ)) / cells)

    for e in range(SWEEPS):
        for d in range(4):
            left(has[d], solid_copy(e, d, e == 0))
    for d in range(4):
        left(has[d], fluid_sent(d))
    for d in range(4):
        left(has[d], con_copy(d))
    left(has_lo_b, wide_copy)
    left(has_lo_b, r0_copy)
    left(has_hi_b, dl_copy)
    for d in (2, 3):
        left(has[d], edge_copy(d))
    spread_waiter(msend, mrecv, 0, 1).wait_send()
    spread_waiter(fsend, frecv, 1, slot - 1).wait_send()
    spread_waiter(rsend, rrecv, 2, slot - 1).wait_send()
    spread_waiter(nmine, nrow, 4, 1).wait_send()
    norm_waiter.wait_send()
    for copy in outs:
        copy.wait()


def write_kernel(adjoint, solid, norms, adjoint_out, solid_out, norms_out, sem):
    copies = [
        pltpu.make_async_copy(adjoint, adjoint_out, sem.at[0]),
        pltpu.make_async_copy(solid, solid_out, sem.at[1]),
    ]
    for copy in copies:
        copy.start()
    norms_out[...] = norms[0, 0 : NF + 1]
    for copy in copies:
        copy.wait()


def shards(
    nb,
    nsp,
    slot,
    fluid_adjoint_in,
    fluid_source,
    velocity,
    diffusion,
    jacobian,
    wall_coefficient,
    metal_costate_prior,
    solid_source,
    conductivity,
    tile_owner,
    tile_target,
):
    ns = nb * slot
    every = nb * nsp

    def stay(x):
        return pltpu.with_memory_space_constraint(x, pltpu.HBM)

    anywhere = pl.BlockSpec(memory_space=pl.ANY)
    vmem = pl.BlockSpec(memory_space=pltpu.VMEM)
    V = pltpu.VMEM
    n40 = CY + 2 * W4
    dma = pltpu.SemaphoreType.DMA
    scratch = [
        pltpu.SMEM((NF,), F32),
        pltpu.SMEM((NF, NF), F32),
        V((1, CY), jnp.int32),
        V((1, CY), jnp.int32),
        V((SWEEPS + 1, NF, CX + 2, ROWS, NZ), F32),
        V((NF, CX, CY, NZ), F32),
        V((3, CX, CY, NZ), F32),
        V((NF, CX, CY, NZ), F32),
        V((CY, NZ), F32),
        V((CY, NZ), F32),
        V((SWEEPS, CH + 2, ROWS, NZ), F32),
        V((CH + 2, ROWS, NZ), F32),
        V((CH, CY, NZ), F32),
        V((CH, CY, NZ), F32),
        V((CH, CY, NZ), F32),
        V((CH, CY, NZ), F32),
        V((CH, CY, NZ), F32),
        V((7, CY, NZ), F32),
        V((3, CY, NZ), F32),
        V((9, ROWS, NZ), F32),
        V((8, n40, NZ), F32),
        V((8, n40, NZ), F32),
        V((8, n40, NZ), F32),
        V((9, ROWS, NZ), F32),
        V((3, 9, ROWS, NZ), F32),
        V((3, CY, NZ), F32),
        V((3, CY, NZ), F32),
        V((ns, CY), jnp.bfloat16),
        V((CY, ns), jnp.bfloat16),
        V((NZ, ns), jnp.bfloat16),
        V((ns, NZ), jnp.bfloat16),
    ]
    scratch += [V((nb, NZ), F32)] * 2
    scratch += [V((ns, NZ), F32)] * 4
    scratch += [V((1, NZ), F32), V((nb, NZ), F32)]
    scratch += [V((1, NZ), F32), V((nsp, 1, NZ), F32)]
    scratch += [
        dma((11,)),
        dma((6,)),
        dma((2,)),
        dma((SWEEPS, 2, len(GROUPS))),
        dma((2,)),
        dma((SWEEPS, 2, len(GROUPS))),
        dma((SWEEPS, 2, len(GROUPS))),
        dma((SWEEPS, 4)),
        dma((SWEEPS, 4)),
        dma((9,)),
        dma((9,)),
        dma((1,)),
        dma((1,)),
        dma((5,)),
        dma((5,)),
        pltpu.SemaphoreType.REGULAR((8,)),
        pltpu.SemaphoreType.REGULAR((8,)),
    ]
    adjoint, solid, norms = pl.pallas_call(
        functools.partial(
            kernel, nb, nsp, slot, float(CX * CY * NZ * every), float(CH * CY * NZ * every)
        ),
        out_shape=(
            jax.ShapeDtypeStruct(fluid_adjoint_in.shape, F32),
            jax.ShapeDtypeStruct(metal_costate_prior.shape, F32),
            jax.ShapeDtypeStruct((8, NZ), F32),
        ),
        in_specs=[anywhere] * 11,
        out_specs=(anywhere, anywhere, vmem),
        scratch_shapes=scratch,
        compiler_params=pltpu.CompilerParams(collective_id=0, has_side_effects=True, vmem_limit_bytes=24 * 2**20),
        name="iteration",
    )(
        *map(
            stay,
            (
                fluid_adjoint_in,
                fluid_source,
                velocity,
                diffusion,
                jacobian,
                wall_coefficient,
                metal_costate_prior,
                solid_source,
                conductivity,
                tile_owner.reshape(1, CY),
                tile_target,
            ),
        )
    )
    hbm = pl.BlockSpec(memory_space=pltpu.HBM)
    return pl.pallas_call(
        write_kernel,
        out_shape=(
            jax.ShapeDtypeStruct(fluid_adjoint_in.shape, F32),
            jax.ShapeDtypeStruct(metal_costate_prior.shape, F32),
            jax.ShapeDtypeStruct((NF + 1,), F32),
        ),
        in_specs=[vmem, vmem, vmem],
        out_specs=(hbm, hbm, vmem),
        scratch_shapes=[dma((2,))],
        compiler_params=pltpu.CompilerParams(vmem_limit_bytes=24 * 2**20),
        name="write",
    )(adjoint, solid, norms)


def solution(mesh, slot=4):
    placed = (
        P(None, "blk", "span", None),
        P(None, "blk", "span", None),
        P(None, "blk", "span", None),
        P(),
        P(),
        P("blk", "span", None),
        P("blk", "span", None),
        P("blk", "span", None),
        P("blk", "span", None),
        P("span", "blk", None),
        P("span", "blk"),
    )
    return jax.shard_map(
        functools.partial(shards, mesh.shape["blk"], mesh.shape["span"], slot),
        mesh=mesh,
        in_specs=placed,
        out_specs=(P(None, "blk", "span", None), P("blk", "span", None), P()),
        check_vma=False,
    )
```
